32 devices in a mesh: band: 4 (over x, core), freq: 8 (over z, y).
Axes of the slice: x: 2, y: 2, z: 4, core: 2. Of those that a mesh axis runs over, the one named last changes fastest.
Arguments:
- spectrum: float32 [8, 36, 64, 64], P('freq', None, 'band'), may hold values from 0.05 to 1
- velocity: float32 [2, 24, 64, 64], P(None, None, 'band', 'freq'), may hold values from -3 to 3
- gain_matrix: bfloat16 [288, 288], replicated, may hold values from -0.375 to 0.375
- quad_matrix: bfloat16 [288, 288], replicated, may hold values from -0.375 to 0.375
- limiter_flags: int32 [8, 64, 64], replicated, may hold values 0 or 1
- sea_mask: int32 [64, 64], replicated, may hold values 0 or 1
- current_route: int32 [8], replicated, may hold values from 0 to 23
- stokes_route: int32 [8, 4], replicated, may hold values from 0 to 23
Outputs:
- spectrum_out: float32 [8, 36, 64, 64], P('freq', None, 'band')
- velocity_out: float32 [2, 24, 64, 64], P(None, None, 'band', 'freq')
The draws below stay inside these ranges and needn't reach their ends.
All inputs are finite; a program needn't handle non-finite values.
Results may differ from the reference program's by a relative error of at most 0.00045.
Values sent between devices are 32-bit elements; how exact they have to be, the bound alone decides.
A program may use at most 64 MiB of HBM per device.

```python
import jax
import jax.numpy as jnp
from jax import lax

DIR = 36
LAT_DEV = 16
LAYERS = 24
SUB = 4
CYCLES = 2
OSTEPS = 3
KS = 4
F = 8
COMP = 288
NLAT = 64
NLON = 64
N_BAND = 4


def place_ends(values, rng, least, top_value):
    place = [jax.random.randint(jax.random.fold_in(rng, axis), (), 0, length) for axis, length in enumerate(values.shape)]
    widest = values.shape.index(max(values.shape))
    next_to = place[:widest] + [(place[widest] + 1) % values.shape[widest]] + place[widest + 1:]
    return values.at[tuple(place)].set(least).at[tuple(next_to)].set(top_value)


def block_scale(stream_key, extent, cuts, least, high):
    loudness, own = 1.0, jax.random.fold_in(stream_key, 6)
    for axis_at, shards_of in cuts:
        heights = jnp.exp(jax.random.uniform(jax.random.fold_in(own, axis_at), (shards_of,), jnp.float32, least / len(cuts), high / len(cuts)))
        loudness = loudness * jnp.repeat(heights, extent[axis_at] // shards_of).reshape([-1 if axis == axis_at else 1 for axis in range(len(extent))])
    return loudness


def scatter_about(rng, dims, deviation, limit, pieces=(), kind=jnp.bfloat16):
    loudness = block_scale(rng, dims, pieces, -0.22, 0.18) if pieces else 1.0
    array = jax.random.normal(rng, dims, jnp.float32) * deviation * loudness
    return jnp.minimum(jnp.maximum(array, -limit), limit).astype(kind)


def setup_inputs(seed: int = 0) -> dict:
    seeds = jax.random.split(jax.random.key(seed), 9)
    spectrum = jnp.clip(0.05 + 0.95 * jax.random.uniform(seeds[0], (F, DIR, NLAT, NLON), jnp.float32) ** block_scale(seeds[0], (F, DIR, NLAT, NLON), ((0, 8), (2, 4)), -0.2, 0.2), 0.05, 1.0)
    velocity = scatter_about(seeds[1], (2, LAYERS, NLAT, NLON), 0.5, 3.0, ((2, 4), (3, 8)), jnp.float32)
    gain_matrix = scatter_about(seeds[2], (COMP, COMP), COMP ** -0.5, 0.375)
    quad_matrix = scatter_about(seeds[3], (COMP, COMP), COMP ** -0.5, 0.375)
    limiter_flags = place_ends((jax.random.randint(seeds[4], (CYCLES * SUB, NLAT, NLON), 0, 2) < 1).astype(jnp.int32), jax.random.fold_in(seeds[4], 1), 0, 1)
    sea_mask = place_ends((jax.random.randint(seeds[5], (NLAT, NLON), 0, 4) < 3).astype(jnp.int32), jax.random.fold_in(seeds[5], 1), 0, 1)
    current_route = place_ends(jax.random.randint(seeds[6], (F,), 0, LAYERS), jax.random.fold_in(seeds[6], 1), 0, LAYERS - 1).astype(jnp.int32)
    stokes_route = place_ends(jax.random.randint(seeds[7], (F, KS), 0, LAYERS), jax.random.fold_in(seeds[7], 1), 0, LAYERS - 1).astype(jnp.int32)
    return dict(spectrum=spectrum, velocity=velocity, gain_matrix=gain_matrix, quad_matrix=quad_matrix, limiter_flags=limiter_flags, sea_mask=sea_mask, current_route=current_route, stokes_route=stokes_route)


precise = lax.Precision.HIGHEST
ocean_dt = 0.2
viscous = 0.5
coriolis = 1.0
mixing = 0.5
friction = 0.1


def directions(how_many):
    angles = (jnp.arange(how_many, dtype=jnp.float32) + 0.5) * (2.0 * jnp.pi / how_many)
    return jnp.cos(angles), jnp.sin(angles)


def speed_of(position, total_count):
    return 0.5 + 0.3 * (position.astype(jnp.float32) + 0.5) / total_count


def wavenumber(position, total_count):
    return 0.5 + 1.5 * (position.astype(jnp.float32) + 0.5) / total_count


def pad_last(values):
    zero_col = jnp.zeros(values.shape[:-1] + (1,), values.dtype)
    return jnp.concatenate([zero_col, values, zero_col], axis=-1)


def transport(lower_side, upper_side, courant, limiter):
    upwind = jnp.maximum(courant, 0.0) * lower_side + jnp.minimum(courant, 0.0) * upper_side
    wendroff = 0.5 * courant * (lower_side + upper_side) - 0.5 * courant * courant * (upper_side - lower_side)
    return upwind + limiter * (wendroff - upwind)


def substep(extended, current, limiter_rows, sea_rows, rate_now, cos_table, sin_table):
    limiter = limiter_rows.astype(jnp.float32)
    drifts = 0.15 * jnp.tanh(current)
    north_drift = drifts[..., 1:2, :, :]
    face_north = 0.5 * (north_drift[..., :-1, :] + north_drift[..., 1:, :])
    courant = rate_now * sin_table[:, None, None] + face_north
    flux_north = transport(extended[..., :-1, :], extended[..., 1:, :], courant, limiter[1:, :])
    shifted = extended[..., 1:-1, :] - (flux_north[..., 1:, :] - flux_north[..., :-1, :])
    east_drift = pad_last(drifts[..., 0:1, 1:-1, :])
    face_east = 0.5 * (east_drift[..., :-1] + east_drift[..., 1:])
    courant_east = rate_now * cos_table[:, None, None] + face_east
    padded = pad_last(shifted)
    limiter_east = pad_last(limiter[1:-1, :])[:, 1:]
    flux_east = transport(padded[..., :-1], padded[..., 1:], courant_east, limiter_east)
    result = shifted - (flux_east[..., 1:] - flux_east[..., :-1])
    return result * sea_rows.astype(jnp.float32)


def source(block, gain_matrix, quad_matrix):
    block_shape = block.shape
    flattened = block.reshape(block_shape[0] * block_shape[1], -1)
    gain_arg = jnp.dot(gain_matrix, flattened.astype(jnp.bfloat16), preferred_element_type=jnp.float32)
    quartic = jnp.dot(quad_matrix, (flattened * flattened).astype(jnp.bfloat16), preferred_element_type=jnp.float32)
    updated = flattened * (1.0 + 0.5 * jnp.tanh(gain_arg) - 0.25 * jnp.tanh(quartic))
    return updated.reshape(block_shape)


def deposit_table(stokes_route):
    layer_ids = jnp.arange(LAYERS, dtype=jnp.int32)
    weights = 1.0 / (1.0 + jnp.arange(stokes_route.shape[1], dtype=jnp.float32))
    hits = (stokes_route[:, :, None] == layer_ids[None, None, :]).astype(jnp.float32)
    return jnp.sum(hits * weights[None, :, None], axis=1)


def stokes_profile(spectrum, numbers, deposit):
    cos_table, sin_table = directions(spectrum.shape[1])
    factor = numbers * (spectrum.shape[1] ** -0.5)
    eastward = jnp.einsum("fdrc,d->frc", spectrum, cos_table, precision=precise) * factor[:, None, None]
    northward = jnp.einsum("fdrc,d->frc", spectrum, sin_table, precision=precise) * factor[:, None, None]
    stacked = jnp.stack([eastward, northward], axis=1)
    return jnp.einsum("fl,fsrc->slrc", deposit, stacked, precision=precise)


def ocean_step(padded, stokes, sea_tile):
    inner = padded[:, :, 1:-1, 1:-1]
    laplace = padded[:, :, 2:, 1:-1] + padded[:, :, :-2, 1:-1] + padded[:, :, 1:-1, 2:] + padded[:, :, 1:-1, :-2] - 4.0 * inner
    vertical = jnp.pad(inner, ((0, 0), (1, 1), (0, 0), (0, 0)))
    mixing_term = vertical[:, 2:] + vertical[:, :-2] - 2.0 * inner
    moving = inner + stokes
    turning = jnp.stack([moving[1], -moving[0]])
    tendency = viscous * laplace + coriolis * turning + mixing * mixing_term - friction * inner
    return (inner + ocean_dt * tendency) * sea_tile.astype(jnp.float32)


def reference(spectrum, velocity, gain_matrix, quad_matrix, limiter_flags, sea_mask, current_route, stokes_route):
    freq_total = spectrum.shape[0]
    cos_table, sin_table = directions(DIR)
    indices = jnp.arange(freq_total, dtype=jnp.int32)
    speeds = speed_of(indices, freq_total)
    numbers = wavenumber(indices, freq_total)
    current = jnp.swapaxes(velocity[:, current_route], 0, 1)
    current_ext = jnp.pad(current, ((0, 0), (0, 0), (1, 1), (0, 0)))
    flag_ext = jnp.pad(limiter_flags, ((0, 0), (1, 1), (0, 0)))
    deposit = deposit_table(stokes_route)
    stokes = jnp.zeros((2, LAYERS) + spectrum.shape[2:], jnp.float32)
    for cycle_index in range(CYCLES):
        def advect(packed):
            field_now, drift_ext, rate_now = packed
            for step_index in range(SUB):
                extended = jnp.pad(field_now, ((0, 0), (1, 1), (0, 0)))
                field_now = substep(extended, drift_ext, flag_ext[cycle_index * SUB + step_index], sea_mask, rate_now, cos_table, sin_table)
            return field_now

        spectrum = lax.map(advect, (spectrum, current_ext, speeds))
        if cycle_index == 0:
            stokes = stokes_profile(spectrum, numbers, deposit)
        blocks = spectrum.reshape(freq_total, DIR, N_BAND, LAT_DEV, spectrum.shape[3])
        blocks = jnp.moveaxis(blocks, 2, 0)
        blocks = lax.map(lambda piece: source(piece, gain_matrix, quad_matrix), blocks)
        spectrum = jnp.moveaxis(blocks, 0, 2).reshape(freq_total, DIR, N_BAND * LAT_DEV, blocks.shape[-1])
    for step_index in range(OSTEPS):
        padded = jnp.pad(velocity, ((0, 0), (0, 0), (1, 1), (1, 1)))
        velocity = ocean_step(padded, stokes, sea_mask)
    return spectrum, velocity
```

```python
import jax
import jax.numpy as jnp
from jax import lax
from jax.sharding import PartitionSpec as P

DIR = 36
F_DEV = 1
LAYERS = 24
SUB = 4
CYCLES = 2
OSTEPS = 3


precise = lax.Precision.HIGHEST
ocean_dt = 0.2
viscous = 0.5
coriolis = 1.0
mixing = 0.5
friction = 0.1


def padded_2(cells, sides, width):
    for axis, dim in sides:
        count = lax.axis_size(axis)
        ends = count - 1
        head = lax.slice_in_dim(cells, 0, width, axis=dim)
        tail = lax.slice_in_dim(cells, cells.shape[dim] - width, cells.shape[dim], axis=dim)
        cells = jnp.concatenate(
            [
                lax.ppermute(tail, axis, [(i, (i + 1) % count) for i in range(ends)]),
                cells,
                lax.ppermute(head, axis, [((i + 1) % count, i) for i in range(ends)]),
            ],
            axis=dim,
        )
    return cells


def directions(how_many):
    angles = (jnp.arange(how_many, dtype=jnp.float32) + 0.5) * (2.0 * jnp.pi / how_many)
    return (jnp.cos(angles), jnp.sin(angles))


def speed_of(position, total_count):
    return 0.5 + 0.3 * (position.astype(jnp.float32) + 0.5) / total_count


def wavenumber(position, total_count):
    return 0.5 + 1.5 * (position.astype(jnp.float32) + 0.5) / total_count


def pad_last(values):
    zero_col = jnp.zeros(values.shape[:-1] + (1,), values.dtype)
    return jnp.concatenate([zero_col, values, zero_col], axis=-1)


def transport(lower_side, upper_side, courant, limiter):
    upwind = jnp.maximum(courant, 0.0) * lower_side + jnp.minimum(courant, 0.0) * upper_side
    wendroff = 0.5 * courant * (lower_side + upper_side) - 0.5 * courant * courant * (
        upper_side - lower_side
    )
    return upwind + limiter * (wendroff - upwind)


def substep(extended, current, limiter_rows, sea_rows, rate_now, cos_table, sin_table):
    limiter = limiter_rows.astype(jnp.float32)
    drifts = 0.15 * jnp.tanh(current)
    north_drift = drifts[..., 1:2, :, :]
    face_north = 0.5 * (north_drift[..., :-1, :] + north_drift[..., 1:, :])
    courant = rate_now * sin_table[:, None, None] + face_north
    flux_north = transport(extended[..., :-1, :], extended[..., 1:, :], courant, limiter[1:, :])
    shifted = extended[..., 1:-1, :] - (flux_north[..., 1:, :] - flux_north[..., :-1, :])
    east_drift = pad_last(drifts[..., 0:1, 1:-1, :])
    face_east = 0.5 * (east_drift[..., :-1] + east_drift[..., 1:])
    courant_east = rate_now * cos_table[:, None, None] + face_east
    padded = pad_last(shifted)
    limiter_east = pad_last(limiter[1:-1, :])[:, 1:]
    flux_east = transport(padded[..., :-1], padded[..., 1:], courant_east, limiter_east)
    result = shifted - (flux_east[..., 1:] - flux_east[..., :-1])
    return result * sea_rows.astype(jnp.float32)


def source(block, gain_matrix, quad_matrix):
    block_shape = block.shape
    flattened = block.reshape(block_shape[0] * block_shape[1], -1)
    gain_arg = jnp.dot(
        gain_matrix, flattened.astype(jnp.bfloat16), preferred_element_type=jnp.float32
    )
    quartic = jnp.dot(
        quad_matrix,
        (flattened * flattened).astype(jnp.bfloat16),
        preferred_element_type=jnp.float32,
    )
    updated = flattened * (1.0 + 0.5 * jnp.tanh(gain_arg) - 0.25 * jnp.tanh(quartic))
    return updated.reshape(block_shape)


def deposit_table(stokes_route):
    layer_ids = jnp.arange(LAYERS, dtype=jnp.int32)
    weights = 1.0 / (1.0 + jnp.arange(stokes_route.shape[1], dtype=jnp.float32))
    hits = (stokes_route[:, :, None] == layer_ids[None, None, :]).astype(jnp.float32)
    return jnp.sum(hits * weights[None, :, None], axis=1)


def stokes_profile(spectrum, numbers, deposit):
    cos_table, sin_table = directions(spectrum.shape[1])
    factor = numbers * spectrum.shape[1] ** (-0.5)
    eastward = (
        jnp.einsum("fdrc,d->frc", spectrum, cos_table, precision=precise) * factor[:, None, None]
    )
    northward = (
        jnp.einsum("fdrc,d->frc", spectrum, sin_table, precision=precise) * factor[:, None, None]
    )
    stacked = jnp.stack([eastward, northward], axis=1)
    return jnp.einsum("fl,fsrc->slrc", deposit, stacked, precision=precise)


def ocean_step(padded, stokes, sea_tile):
    inner = padded[:, :, 1:-1, 1:-1]
    laplace = (
        padded[:, :, 2:, 1:-1]
        + padded[:, :, :-2, 1:-1]
        + padded[:, :, 1:-1, 2:]
        + padded[:, :, 1:-1, :-2]
        - 4.0 * inner
    )
    vertical = jnp.pad(inner, ((0, 0), (1, 1), (0, 0), (0, 0)))
    mixing_term = vertical[:, 2:] + vertical[:, :-2] - 2.0 * inner
    moving = inner + stokes
    turning = jnp.stack([moving[1], -moving[0]])
    tendency = viscous * laplace + coriolis * turning + mixing * mixing_term - friction * inner
    return (inner + ocean_dt * tendency) * sea_tile.astype(jnp.float32)


def ocean_steps(wide, drift_wide, sea_wide):
    for step_index in range(OSTEPS):
        rows, cols = wide.shape[2] - 2, wide.shape[3] - 2
        trim = step_index
        drift = drift_wide[:, :, trim : trim + rows, trim : trim + cols]
        wide = ocean_step(wide, drift, sea_wide[trim : trim + rows, trim : trim + cols])
    return wide


def body(
    spectrum,
    velocity,
    gain_matrix,
    quad_matrix,
    limiter_flags,
    sea_mask,
    current_route,
    stokes_route,
):
    band_index = lax.axis_index("band")
    freq_index = lax.axis_index("freq")
    freq_count = lax.axis_size("freq")
    freq_total = F_DEV * freq_count
    local_rows = spectrum.shape[2]
    grid_cols = spectrum.shape[3]
    tile_cols = velocity.shape[3]
    edge = OSTEPS - 1
    deep = SUB + edge
    cos_table, sin_table = directions(DIR)
    rate_now = speed_of(freq_index, freq_total)
    number_now = wavenumber(freq_index, freq_total)
    deposit_all = deposit_table(stokes_route)
    layer_ids = jnp.arange(LAYERS, dtype=jnp.int32)
    picker = (current_route[:, None] == layer_ids[None, :]).astype(jnp.float32)
    outgoing = jnp.einsum("fl,slrc->fsrc", picker, velocity, precision=precise)
    current = lax.all_to_all(outgoing, "freq", split_axis=0, concat_axis=3, tiled=True)[0]
    wide_ocean = padded_2(velocity, (("band", 2), ("freq", 3)), OSTEPS)
    both = jnp.concatenate([spectrum[0], current], axis=0)
    both = padded_2(both, (("band", 1),), deep)
    field, current = both[:DIR], both[DIR:]
    flag_pad = jnp.pad(limiter_flags, ((0, 0), (deep, deep), (0, 0)))
    flag_rows = lax.dynamic_slice_in_dim(
        flag_pad, band_index * local_rows, local_rows + 2 * deep, 1
    )
    sea_rows = lax.dynamic_slice_in_dim(
        jnp.pad(sea_mask, ((deep, deep), (0, 0))), band_index * local_rows, local_rows + 2 * deep, 0
    )

    def advect(extended, cycle_index, depth):
        for step_index in range(SUB):
            low = deep - depth + step_index
            high = local_rows + 2 * deep - low
            extended = substep(
                extended,
                current[:, low:high],
                flag_rows[cycle_index * SUB + step_index, low:high],
                sea_rows[low + 1 : high - 1],
                rate_now,
                cos_table,
                sin_table,
            )
        return extended

    def send_out(rows_of):
        return lax.all_to_all(rows_of, "freq", split_axis=1, concat_axis=0, tiled=False)

    def send_back(whole):
        moved = lax.all_to_all(
            whole.reshape(freq_count, DIR, -1), "freq", split_axis=0, concat_axis=1, tiled=False
        )
        return moved.reshape(DIR, local_rows, grid_cols)

    field = advect(field, 0, deep)
    factor = number_now * DIR ** (-0.5)
    moments = jnp.stack(
        [
            jnp.sum(field * cos_table[:, None, None], axis=0),
            jnp.sum(field * sin_table[:, None, None], axis=0),
        ]
    ) * factor
    moments = jnp.pad(moments, ((0, 0), (0, 0), (edge, edge)))
    span = tile_cols + 2 * edge
    windows = jnp.stack(
        [moments[:, :, j * tile_cols : j * tile_cols + span] for j in range(freq_count)]
    )
    cells = local_rows * grid_cols // freq_count
    size = 2 * (local_rows + 2 * edge) * span
    extra = -(-size // cells)
    windows = jnp.pad(windows.reshape(freq_count, size), ((0, 0), (0, extra * cells - size)))
    windows = jnp.transpose(windows.reshape(freq_count, extra, cells), (1, 0, 2))
    grouped = field[:, edge : edge + local_rows].reshape(DIR, freq_count, cells)
    arrived = send_out(jnp.concatenate([grouped, windows], axis=0))
    whole = source(arrived[:, :DIR], gain_matrix, quad_matrix)
    stacked = arrived[:, DIR:].reshape(freq_count, extra * cells)[:, :size]
    stacked = stacked.reshape(freq_count, 2, local_rows + 2 * edge, span)
    drift_wide = jnp.einsum("fl,fsrc->slrc", deposit_all, stacked, precision=precise)
    sea_wide = lax.dynamic_slice(
        jnp.pad(sea_mask, edge),
        (band_index * local_rows, freq_index * tile_cols),
        (local_rows + 2 * edge, span),
    )
    ocean_now = ocean_steps(wide_ocean, drift_wide, sea_wide)
    for cycle_index in range(1, CYCLES):
        field = padded_2(send_back(whole), (("band", 1),), SUB)
        field = advect(field, cycle_index, SUB)
        arrived = send_out(field.reshape(DIR, freq_count, cells))
        whole = source(arrived, gain_matrix, quad_matrix)
    return (send_back(whole)[None], ocean_now)


def solution(mesh):
    return jax.shard_map(
        body,
        mesh=mesh,
        in_specs=(
            P("freq", None, "band", None),
            P(None, None, "band", "freq"),
            P(),
            P(),
            P(),
            P(),
            P(),
            P(),
        ),
        out_specs=(P("freq", None, "band", None), P(None, None, "band", "freq")),
        check_vma=False,
    )
```

```python
import functools

import jax
import jax.numpy as jnp
from jax import lax
from jax.experimental import pallas as pl
from jax.experimental.pallas import tpu as pltpu
from jax.sharding import PartitionSpec as P

DIR = 36
F_DEV = 1
LAYERS = 24
SUB = 4
CYCLES = 2
OSTEPS = 3


precise = lax.Precision.HIGHEST
ocean_dt = 0.2
viscous = 0.5
coriolis = 1.0
mixing = 0.5
friction = 0.1


def directions(how_many):
    angles = (jnp.arange(how_many, dtype=jnp.float32) + 0.5) * (2.0 * jnp.pi / how_many)
    return (jnp.cos(angles), jnp.sin(angles))


def speed_of(position, total_count):
    return 0.5 + 0.3 * (position.astype(jnp.float32) + 0.5) / total_count


def wavenumber(position, total_count):
    return 0.5 + 1.5 * (position.astype(jnp.float32) + 0.5) / total_count


def deposit_table(stokes_route):
    layer_ids = jnp.arange(LAYERS, dtype=jnp.int32)
    weights = 1.0 / (1.0 + jnp.arange(stokes_route.shape[1], dtype=jnp.float32))
    hits = (stokes_route[:, :, None] == layer_ids[None, None, :]).astype(jnp.float32)
    return jnp.sum(hits * weights[None, :, None], axis=1)


def ocean_step(padded, stokes, sea_tile):
    inner = padded[:, :, 1:-1, 1:-1]
    laplace = (
        padded[:, :, 2:, 1:-1]
        + padded[:, :, :-2, 1:-1]
        + padded[:, :, 1:-1, 2:]
        + padded[:, :, 1:-1, :-2]
        - 4.0 * inner
    )
    vertical = jnp.pad(inner, ((0, 0), (1, 1), (0, 0), (0, 0)))
    mixing_term = vertical[:, 2:] + vertical[:, :-2] - 2.0 * inner
    moving = inner + stokes
    turning = jnp.stack([moving[1], -moving[0]])
    tendency = viscous * laplace + coriolis * turning + mixing * mixing_term - friction * inner
    return (inner + ocean_dt * tendency) * sea_tile.astype(jnp.float32)


EDGE = OSTEPS - 1
DEEP = SUB + EDGE
MESH = pl.DeviceIdType.MESH


def advect(state, table, face_flags, sea, first, last, drift_north, drift_east, cols):
    lanes = state.shape[1]
    up = lanes - cols
    rate_east, rate_north = table[:, 0:1], table[:, 1:2]
    inner = 1.0 - last

    def parts(courant):
        size = jnp.abs(courant)
        return 0.5 * courant, 0.5 * size, 0.5 * (courant * courant - size)

    north = parts(rate_north + 0.5 * (drift_north + pltpu.roll(drift_north, up, 1)))
    east = parts(rate_east + 0.5 * (drift_east + inner * pltpu.roll(drift_east, lanes - 1, 1)))
    west = parts(rate_east + 0.5 * drift_east)
    west_base = first * (west[0] - west[1])
    west_more = first * west[2]
    for step_index in range(SUB):
        flags = face_flags[step_index : step_index + 1]
        flag_north = pltpu.roll(flags, up, 1)
        flag_east = inner * pltpu.roll(flags, lanes - 1, 1)
        above = pltpu.roll(state, up, 1)
        flux = north[0] * (state + above) + (north[1] + flag_north * north[2]) * (state - above)
        state = state - (flux - pltpu.roll(flux, cols, 1))
        beside = inner * pltpu.roll(state, lanes - 1, 1)
        flux = east[0] * (state + beside) + (east[1] + flag_east * east[2]) * (state - beside)
        lower = (1.0 - first) * pltpu.roll(flux, 1, 1) + state * (west_base - flags * west_more)
        state = (state - (flux - lower)) * sea
    return state


def kernel(
    bands,
    freqs,
    cols,
    route,
    spectrum,
    placed,
    tile,
    gain_matrix,
    quad_matrix,
    masks,
    table,
    result,
    moments_out,
    tiles_out,
    wide,
    route_out,
    route_own,
    route_low,
    route_high,
    leave,
    arrive,
    back,
    again,
    moments_send,
    moments,
    tiles,
    drift,
    final,
    halo_sems,
    route_sems,
    edge_route_sems,
    tile_sems,
    out_sems,
    moment_sems,
    back_sems,
    edge_sems,
):
    band = lax.axis_index("band")
    me = lax.axis_index("freq")
    cells = spectrum.shape[1]
    chunk = cells // freqs
    deep = DEEP * cols
    near = SUB * cols
    edges = near // chunk
    has_low = band > 0
    has_high = band < bands - 1

    def others(fn):
        def step(i, carry):
            fn(lax.rem(me + i, freqs))
            return carry

        lax.fori_loop(1, freqs, step, 0)

    def every(fn):
        def step(i, carry):
            fn(i)
            return carry

        lax.fori_loop(0, freqs, step, 0)

    def copy(src, dst, sems, slot_send, slot_recv, to_band, to_freq):
        return pltpu.make_async_remote_copy(
            src_ref=src,
            dst_ref=dst,
            send_sem=sems.at[(0,) + slot_send],
            recv_sem=sems.at[(1,) + slot_recv],
            device_id=(to_band, to_freq),
            device_id_type=MESH,
        )

    barrier = pltpu.get_barrier_semaphore()

    def greet(to_band, to_freq):
        pl.semaphore_signal(barrier, inc=1, device_id=(to_band, to_freq), device_id_type=MESH)

    others(lambda f: greet(band, f))

    @pl.when(has_low)
    def _():
        every(lambda f: greet(band - 1, f))

    @pl.when(has_high)
    def _():
        every(lambda f: greet(band + 1, f))

    def prepare(f):
        route_out[f] = placed[route[f]]

    every(prepare)
    count = freqs - 1 + freqs * (has_low.astype(jnp.int32) + has_high.astype(jnp.int32))
    pl.semaphore_wait(barrier, count)

    halo_low = copy(
        spectrum.at[:, pl.ds(0, deep)],
        wide.at[:, pl.ds(deep + cells, deep)],
        halo_sems,
        (0,),
        (0,),
        band - 1,
        me,
    )
    halo_high = copy(
        spectrum.at[:, pl.ds(cells - deep, deep)],
        wide.at[:, pl.ds(0, deep)],
        halo_sems,
        (1,),
        (1,),
        band + 1,
        me,
    )

    def route_copy(f):
        return copy(route_out.at[f], route_own.at[me], route_sems, (f,), (me,), band, f)

    def route_to_low(f):
        return copy(
            route_out.at[f, :, pl.ds(0, deep)], route_high.at[me], edge_route_sems,
            (0, f), (0, me), band - 1, f,
        )

    def route_to_high(f):
        return copy(
            route_out.at[f, :, pl.ds(cells - deep, deep)], route_low.at[me], edge_route_sems,
            (1, f), (1, me), band + 1, f,
        )

    others(lambda f: route_copy(f).start())

    @pl.when(has_low)
    def _():
        every(lambda f: route_to_low(f).start())
        halo_low.start()

    @pl.when(has_high)
    def _():
        every(lambda f: route_to_high(f).start())
        halo_high.start()

    def near_tiles(fn):
        for down in (-1, 0, 1):
            for side in (-1, 0, 1):
                if down == 0 and side == 0:
                    continue
                to_band, to_freq = band + down, me + side
                there = (to_band >= 0) & (to_band < bands) & (to_freq >= 0) & (to_freq < freqs)
                mine = 3 * (1 + down) + 1 + side
                fn(there, mine, 8 - mine, to_band, to_freq)

    def tile_copy(mine, theirs, to_band, to_freq):
        return copy(tile, tiles.at[theirs], tile_sems, (mine,), (theirs,), to_band, to_freq)

    def tile_start(there, mine, theirs, to_band, to_freq):
        @pl.when(there)
        def _():
            tile_copy(mine, theirs, to_band, to_freq).start()

        @pl.when(jnp.logical_not(there))
        def _():
            tiles[mine] = jnp.zeros_like(tile)

    near_tiles(tile_start)
    tiles[4] = tile[...]
    wide[:, deep : deep + cells] = spectrum[...]
    route_own[me] = route_out[me]

    @pl.when(jnp.logical_not(has_low))
    def _():
        wide[:, :deep] = jnp.zeros((DIR, deep), jnp.float32)
        route_low[...] = jnp.zeros_like(route_low)
        again[:, :near] = jnp.zeros((DIR, near), jnp.float32)

    @pl.when(jnp.logical_not(has_high))
    def _():
        wide[:, deep + cells :] = jnp.zeros((DIR, deep), jnp.float32)
        route_high[...] = jnp.zeros_like(route_high)
        again[:, near + cells :] = jnp.zeros((DIR, near), jnp.float32)

    others(lambda f: copy(
        route_out.at[f], route_own.at[f], route_sems, (f,), (f,), band, f
    ).wait_recv())

    @pl.when(has_low)
    def _():
        every(lambda f: copy(
            route_out.at[f, :, pl.ds(cells - deep, deep)], route_low.at[f], edge_route_sems,
            (1, f), (1, f), band - 1, f,
        ).wait_recv())
        halo_high.wait_recv()

    @pl.when(has_high)
    def _():
        every(lambda f: copy(
            route_out.at[f, :, pl.ds(0, deep)], route_high.at[f], edge_route_sems,
            (0, f), (0, f), band + 1, f,
        ).wait_recv())
        halo_low.wait_recv()

    drift[:, :deep] = 0.15 * jnp.tanh(jnp.sum(route_low[...], axis=0))
    drift[:, deep : deep + cells] = 0.15 * jnp.tanh(jnp.sum(route_own[...], axis=0))
    drift[:, deep + cells :] = 0.15 * jnp.tanh(jnp.sum(route_high[...], axis=0))
    groups = [(low, min(low + 8, DIR)) for low in range(0, DIR, 8)]

    def cycle(source_ref, cycle_index, skip, keep):
        span = source_ref.shape[1]
        window = slice(skip, skip + span)
        shape = (1, span)
        sea = masks[SUB * CYCLES : SUB * CYCLES + 1, window]
        first = masks[SUB * CYCLES + 1 : SUB * CYCLES + 2, window]
        last = masks[SUB * CYCLES + 2 : SUB * CYCLES + 3, window]
        flags = masks[SUB * cycle_index : SUB * (cycle_index + 1), window]
        drift_east, drift_north = drift[0:1, window], drift[1:2, window]
        for low, high in groups:
            state = advect(
                source_ref[low:high, :], table[low:high, :], flags, sea, first, last,
                drift_north, drift_east, cols,
            )
            keep(low, high, state)

    def send_out(index):
        def out_copy(f):
            return copy(
                leave.at[index, :, pl.ds(pl.multiple_of(f * chunk, chunk), chunk)],
                arrive.at[index, me], out_sems, (index, f), (index, me), band, f,
            )

        others(lambda f: out_copy(f).start())
        arrive[index, me] = leave[index, :, pl.ds(pl.multiple_of(me * chunk, chunk), chunk)]

    def wait_out(index):
        others(lambda f: copy(
            leave.at[index, :, pl.ds(0, chunk)], arrive.at[index, f], out_sems,
            (index, f), (index, f), band, f,
        ).wait_recv())

    def source(index):
        whole = jnp.concatenate([arrive[index, f] for f in range(freqs)], axis=0)
        gain = jnp.dot(
            gain_matrix[...], whole.astype(jnp.bfloat16), preferred_element_type=jnp.float32
        )
        quartic = jnp.dot(
            quad_matrix[...],
            (whole * whole).astype(jnp.bfloat16),
            preferred_element_type=jnp.float32,
        )
        updated = whole * (1.0 + 0.5 * jnp.tanh(gain) - 0.25 * jnp.tanh(quartic))
        for f in range(freqs):
            back[index, f] = updated[f * DIR : (f + 1) * DIR]

    def place(ref, start, number):
        return ref.at[:, pl.ds(pl.multiple_of(start + number * chunk, chunk), chunk)]

    def send_back(index, ref, start):
        others(lambda f: copy(
            back.at[index, f], place(ref, start, me), back_sems,
            (index, f), (index, me), band, f,
        ).start())
        ref[:, pl.ds(pl.multiple_of(start + me * chunk, chunk), chunk)] = back[index, me]

    def wait_back(index, ref, start):
        others(lambda f: copy(
            back.at[index, f], place(ref, start, f), back_sems,
            (index, f), (index, f), band, f,
        ).wait_recv())

    def keep_first(low, high, state):
        leave[0, low:high, :] = state[:, deep : deep + cells]
        shown = state[:, near : near + cells + 2 * (deep - near)]
        east = jnp.sum(shown * table[low:high, 2:3], axis=0, keepdims=True)
        north = jnp.sum(shown * table[low:high, 3:4], axis=0, keepdims=True)
        if low == 0:
            moments_send[0:1, :] = east
            moments_send[1:2, :] = north
        else:
            moments_send[0:1, :] += east
            moments_send[1:2, :] += north

    def keep_last(low, high, state):
        leave[1, low:high, :] = state[:, near : near + cells]

    def moment_copy(f):
        return copy(moments_send, moments.at[me], moment_sems, (f,), (me,), band, f)

    cycle(wide, 0, 0, keep_first)
    send_out(0)
    others(lambda f: moment_copy(f).start())
    moments[me] = moments_send[...]
    wait_out(0)
    source(0)

    def edge_low(f):
        return copy(
            back.at[0, f], place(again, near + cells, me), edge_sems,
            (0, f), (0, me), band - 1, f,
        )

    def edge_high(f):
        return copy(
            back.at[0, f], place(again, 0, me - (freqs - edges)), edge_sems,
            (1, f), (1, me), band + 1, f,
        )

    sends_low = has_low & (me < edges)
    sends_high = has_high & (me >= freqs - edges)

    @pl.when(sends_low)
    def _():
        every(lambda f: edge_low(f).start())

    @pl.when(sends_high)
    def _():
        every(lambda f: edge_high(f).start())

    send_back(0, again, near)

    def tile_wait(there, mine, theirs, to_band, to_freq):
        @pl.when(there)
        def _():
            copy(tile, tiles.at[mine], tile_sems, (mine,), (mine,), to_band, to_freq).wait_recv()

    near_tiles(tile_wait)
    tiles_out[...] = tiles[...]
    others(lambda f: copy(
        moments_send, moments.at[f], moment_sems, (f,), (f,), band, f
    ).wait_recv())
    moments_out[...] = moments[...]
    wait_back(0, again, near)

    @pl.when(has_low)
    def _():
        for number in range(edges):
            copy(
                back.at[0, 0], place(again, 0, number), edge_sems,
                (1, 0), (1, freqs - edges + number), band - 1, freqs - edges + number,
            ).wait_recv()

    @pl.when(has_high)
    def _():
        for number in range(edges):
            copy(
                back.at[0, 0], place(again, near + cells, number), edge_sems,
                (0, 0), (0, number), band + 1, number,
            ).wait_recv()

    cycle(again, 1, deep - near, keep_last)
    send_out(1)
    wait_out(1)
    source(1)
    send_back(1, final, 0)

    others(lambda f: route_copy(f).wait_send())
    others(lambda f: moment_copy(f).wait_send())

    @pl.when(has_low)
    def _():
        every(lambda f: route_to_low(f).wait_send())
        halo_low.wait_send()

    @pl.when(has_high)
    def _():
        every(lambda f: route_to_high(f).wait_send())
        halo_high.wait_send()

    def tile_sent(there, mine, theirs, to_band, to_freq):
        @pl.when(there)
        def _():
            tile_copy(mine, theirs, to_band, to_freq).wait_send()

    near_tiles(tile_sent)

    @pl.when(sends_low)
    def _():
        every(lambda f: edge_low(f).wait_send())

    @pl.when(sends_high)
    def _():
        every(lambda f: edge_high(f).wait_send())

    for index in range(CYCLES):
        others(lambda f: copy(
            leave.at[index, :, pl.ds(0, chunk)], arrive.at[index, me], out_sems,
            (index, f), (index, me), band, f,
        ).wait_send())
    wait_back(1, final, 0)
    result[...] = final[...]
    others(lambda f: copy(
        back.at[0, f], place(again, near, me), back_sems, (0, f), (0, me), band, f
    ).wait_send())
    others(lambda f: copy(
        back.at[1, f], place(final, 0, me), back_sems, (1, f), (1, me), band, f
    ).wait_send())


def body(
    spectrum,
    velocity,
    gain_matrix,
    quad_matrix,
    limiter_flags,
    sea_mask,
    current_route,
    stokes_route,
):
    bands = lax.axis_size("band")
    freqs = lax.axis_size("freq")
    band = lax.axis_index("band")
    me = lax.axis_index("freq")
    rows, cols = spectrum.shape[2:]
    tile_cols = velocity.shape[3]
    cells = rows * cols
    chunk = cells // freqs
    edges = SUB * cols // chunk
    assert CYCLES == 2 and cells % freqs == 0 and chunk % 128 == 0
    assert rows >= DEEP and edges * chunk == SUB * cols and edges <= freqs
    assert tile_cols >= OSTEPS and (EDGE * cols) % 128 == 0
    cos_table, sin_table = directions(DIR)
    rate = speed_of(me, freqs)
    factor = wavenumber(me, freqs) * DIR ** (-0.5)
    table = jnp.stack(
        [rate * cos_table, rate * sin_table, factor * cos_table, factor * sin_table], axis=1
    )
    grid = jnp.concatenate([limiter_flags, sea_mask[None]], axis=0)
    grid = jnp.pad(grid, ((0, 0), (DEEP, DEEP), (0, 0)))
    grid = lax.dynamic_slice_in_dim(grid, band * rows, rows + 2 * DEEP, 1)
    at_col = jnp.broadcast_to(jnp.arange(cols), grid.shape[1:])
    sides = jnp.stack([at_col == 0, at_col == cols - 1]).astype(jnp.int32)
    masks = jnp.concatenate([grid, sides], axis=0).astype(jnp.float32)
    masks = masks.reshape(masks.shape[0], -1)
    placed = lax.dynamic_update_slice(
        jnp.zeros((2, LAYERS, rows, cols), jnp.float32), velocity, (0, 0, 0, me * tile_cols)
    )
    placed = jnp.swapaxes(placed, 0, 1).reshape(LAYERS, 2, cells)
    tile_cells = rows * tile_cols
    tile = velocity.reshape(2 * LAYERS, tile_cells)
    shown = (rows + 2 * EDGE) * cols
    deep = DEEP * cols
    f32 = jnp.float32
    vmem = pl.BlockSpec(memory_space=pltpu.VMEM)
    dma = pltpu.SemaphoreType.DMA
    result, moments, tiles = pl.pallas_call(
        functools.partial(kernel, bands, freqs, cols),
        out_shape=(
            jax.ShapeDtypeStruct((DIR, cells), f32),
            jax.ShapeDtypeStruct((freqs, 2, shown), f32),
            jax.ShapeDtypeStruct((9, 2 * LAYERS, tile_cells), f32),
        ),
        in_specs=[pl.BlockSpec(memory_space=pltpu.SMEM)] + [vmem] * 7,
        out_specs=(vmem, vmem, vmem),
        scratch_shapes=[
            pltpu.VMEM((DIR, cells + 2 * deep), f32),
            pltpu.VMEM((freqs, 2, cells), f32),
            pltpu.VMEM((freqs, 2, cells), f32),
            pltpu.VMEM((freqs, 2, deep), f32),
            pltpu.VMEM((freqs, 2, deep), f32),
            pltpu.VMEM((CYCLES, DIR, cells), f32),
            pltpu.VMEM((CYCLES, freqs, DIR, chunk), f32),
            pltpu.VMEM((CYCLES, freqs, DIR, chunk), f32),
            pltpu.VMEM((DIR, cells + 2 * SUB * cols), f32),
            pltpu.VMEM((2, shown), f32),
            pltpu.VMEM((freqs, 2, shown), f32),
            pltpu.VMEM((9, 2 * LAYERS, tile_cells), f32),
            pltpu.VMEM((2, cells + 2 * deep), f32),
            pltpu.VMEM((DIR, cells), f32),
            dma((2, 2)),
            dma((2, freqs)),
            dma((2, 2, freqs)),
            dma((2, 9)),
            dma((2, CYCLES, freqs)),
            dma((2, freqs)),
            dma((2, CYCLES, freqs)),
            dma((2, 2, freqs)),
        ],
        compiler_params=pltpu.CompilerParams(
            collective_id=0, has_side_effects=True, vmem_limit_bytes=60 * 1024 * 1024
        ),
    )(
        current_route,
        spectrum.reshape(DIR, cells),
        placed,
        tile,
        gain_matrix,
        quad_matrix,
        masks,
        table,
    )
    span = tile_cols + 2 * EDGE
    moments = moments.reshape(freqs, 2, rows + 2 * EDGE, cols)
    moments = jnp.pad(moments, ((0, 0), (0, 0), (0, 0), (EDGE, EDGE)))
    moments = lax.dynamic_slice_in_dim(moments, me * tile_cols, span, 3)
    drift = jnp.einsum(
        "fl,fsrc->slrc", deposit_table(stokes_route), moments, precision=precise
    )
    tiles = tiles.reshape(3, 3, 2, LAYERS, rows, tile_cols)
    strips = [
        jnp.concatenate(
            [tiles[0, k][:, :, rows - OSTEPS :], tiles[1, k], tiles[2, k][:, :, :OSTEPS]], axis=2
        )
        for k in range(3)
    ]
    ocean = jnp.concatenate(
        [strips[0][..., tile_cols - OSTEPS :], strips[1], strips[2][..., :OSTEPS]], axis=3
    )
    sea_wide = lax.dynamic_slice(
        jnp.pad(sea_mask, EDGE), (band * rows, me * tile_cols), (rows + 2 * EDGE, span)
    )
    for step_index in range(OSTEPS):
        high, wide = ocean.shape[2] - 2, ocean.shape[3] - 2
        trim = step_index
        ocean = ocean_step(
            ocean,
            drift[:, :, trim : trim + high, trim : trim + wide],
            sea_wide[trim : trim + high, trim : trim + wide],
        )
    return (result.reshape(1, DIR, rows, cols), ocean)


def solution(mesh):
    return jax.shard_map(
        body,
        mesh=mesh,
        in_specs=(
            P("freq", None, "band", None),
            P(None, None, "band", "freq"),
            P(),
            P(),
            P(),
            P(),
            P(),
            P(),
        ),
        out_specs=(P("freq", None, "band", None), P(None, None, "band", "freq")),
        check_vma=False,
    )
```

```python
import functools

import jax
import jax.numpy as jnp
import numpy as np
from jax import lax
from jax.experimental import pallas as pl
from jax.experimental.pallas import tpu as pltpu
from jax.sharding import PartitionSpec as P

DIR = 36
F_DEV = 1
LAYERS = 24
SUB = 4
CYCLES = 2
OSTEPS = 3


precise = lax.Precision.HIGHEST
ocean_dt = 0.2
viscous = 0.5
coriolis = 1.0
mixing = 0.5
friction = 0.1


def deposit_table(stokes_route):
    layer_ids = jnp.arange(LAYERS, dtype=jnp.int32)
    weights = 1.0 / (1.0 + jnp.arange(stokes_route.shape[1], dtype=jnp.float32))
    hits = (stokes_route[:, :, None] == layer_ids[None, None, :]).astype(jnp.float32)
    return jnp.sum(hits * weights[None, :, None], axis=1)


def ocean_step(padded, stokes, sea_tile):
    inner = padded[:, :, 1:-1, 1:-1]
    laplace = (
        padded[:, :, 2:, 1:-1]
        + padded[:, :, :-2, 1:-1]
        + padded[:, :, 1:-1, 2:]
        + padded[:, :, 1:-1, :-2]
        - 4.0 * inner
    )
    vertical = jnp.pad(inner, ((0, 0), (1, 1), (0, 0), (0, 0)))
    mixing_term = vertical[:, 2:] + vertical[:, :-2] - 2.0 * inner
    moving = inner + stokes
    turning = jnp.stack([moving[1], -moving[0]])
    tendency = viscous * laplace + coriolis * turning + mixing * mixing_term - friction * inner
    return (inner + ocean_dt * tendency) * sea_tile.astype(jnp.float32)


EDGE = OSTEPS - 1
DEEP = SUB + EDGE
MESH = pl.DeviceIdType.MESH


def advect(state, table, face_flags, sea, first, last, drift_north, drift_east, cols):
    lanes = state.shape[1]
    up = lanes - cols
    rate_east, rate_north = table[:, 0:1], table[:, 1:2]
    inner = 1.0 - last

    def parts(courant):
        size = jnp.abs(courant)
        return 0.5 * courant, 0.5 * size, 0.5 * (courant * courant - size)

    north = parts(rate_north + 0.5 * (drift_north + pltpu.roll(drift_north, up, 1)))
    east = parts(rate_east + 0.5 * (drift_east + inner * pltpu.roll(drift_east, lanes - 1, 1)))
    west = parts(rate_east + 0.5 * drift_east)
    west_base = first * (west[0] - west[1])
    west_more = first * west[2]
    for step_index in range(SUB):
        flags = face_flags[step_index : step_index + 1]
        flag_north = pltpu.roll(flags, up, 1)
        flag_east = inner * pltpu.roll(flags, lanes - 1, 1)
        above = pltpu.roll(state, up, 1)
        flux = north[0] * (state + above) + (north[1] + flag_north * north[2]) * (state - above)
        state = state - (flux - pltpu.roll(flux, cols, 1))
        beside = inner * pltpu.roll(state, lanes - 1, 1)
        flux = east[0] * (state + beside) + (east[1] + flag_east * east[2]) * (state - beside)
        lower = (1.0 - first) * pltpu.roll(flux, 1, 1) + state * (west_base - flags * west_more)
        state = (state - (flux - lower)) * sea
    return state


def kernel(
    bands,
    freqs,
    cols,
    route,
    spectrum,
    tile,
    gain_matrix,
    quad_matrix,
    masks,
    base,
    result,
    moments_out,
    tiles_out,
    wide,
    route_out,
    route_own,
    route_low,
    route_high,
    table,
    leave,
    arrive,
    back,
    again,
    moments_send,
    moments,
    tiles,
    drift,
    final,
    halo_sems,
    route_sems,
    edge_route_sems,
    tile_sems,
    out_sems,
    moment_sems,
    back_sems,
    edge_sems,
):
    band = lax.axis_index("band")
    me = lax.axis_index("freq")
    cells = spectrum.shape[1]
    chunk = cells // freqs
    deep = DEEP * cols
    near = SUB * cols
    edges = near // chunk
    has_low = band > 0
    has_high = band < bands - 1

    def others(fn):
        def step(i, carry):
            fn(lax.rem(me + i, freqs))
            return carry

        lax.fori_loop(1, freqs, step, 0)

    def every(fn):
        def step(i, carry):
            fn(i)
            return carry

        lax.fori_loop(0, freqs, step, 0)

    def copy(src, dst, sems, slot_send, slot_recv, to_band, to_freq):
        return pltpu.make_async_remote_copy(
            src_ref=src,
            dst_ref=dst,
            send_sem=sems.at[(0,) + slot_send],
            recv_sem=sems.at[(1,) + slot_recv],
            device_id=(to_band, to_freq),
            device_id_type=MESH,
        )

    barrier = pltpu.get_barrier_semaphore()

    def greet(to_band, to_freq):
        pl.semaphore_signal(barrier, inc=1, device_id=(to_band, to_freq), device_id_type=MESH)

    others(lambda f: greet(band, f))

    @pl.when(has_low)
    def _():
        every(lambda f: greet(band - 1, f))

    @pl.when(has_high)
    def _():
        every(lambda f: greet(band + 1, f))

    def prepare(f):
        route_out[f, 0:1, :] = tile[pl.ds(route[f], 1), :]
        route_out[f, 1:2, :] = tile[pl.ds(LAYERS + route[f], 1), :]

    every(prepare)
    count = freqs - 1 + freqs * (has_low.astype(jnp.int32) + has_high.astype(jnp.int32))
    pl.semaphore_wait(barrier, count)

    halo_low = copy(
        spectrum.at[:, pl.ds(0, deep)],
        wide.at[:, pl.ds(deep + cells, deep)],
        halo_sems,
        (0,),
        (0,),
        band - 1,
        me,
    )
    halo_high = copy(
        spectrum.at[:, pl.ds(cells - deep, deep)],
        wide.at[:, pl.ds(0, deep)],
        halo_sems,
        (1,),
        (1,),
        band + 1,
        me,
    )

    def route_copy(f):
        return copy(route_out.at[f], route_own.at[me], route_sems, (f,), (me,), band, f)

    def route_to_low(f):
        return copy(
            route_out.at[f], route_high.at[me], edge_route_sems,
            (0, f), (0, me), band - 1, f,
        )

    def route_to_high(f):
        return copy(
            route_out.at[f], route_low.at[me], edge_route_sems,
            (1, f), (1, me), band + 1, f,
        )

    others(lambda f: route_copy(f).start())

    @pl.when(has_low)
    def _():
        every(lambda f: route_to_low(f).start())
        halo_low.start()

    @pl.when(has_high)
    def _():
        every(lambda f: route_to_high(f).start())
        halo_high.start()

    def near_tiles(fn):
        for down in (-1, 0, 1):
            for side in (-1, 0, 1):
                if down == 0 and side == 0:
                    continue
                to_band, to_freq = band + down, me + side
                there = (to_band >= 0) & (to_band < bands) & (to_freq >= 0) & (to_freq < freqs)
                mine = 3 * (1 + down) + 1 + side
                fn(there, mine, 8 - mine, to_band, to_freq)

    def tile_copy(mine, theirs, to_band, to_freq):
        return copy(tile, tiles.at[theirs], tile_sems, (mine,), (theirs,), to_band, to_freq)

    def tile_start(there, mine, theirs, to_band, to_freq):
        @pl.when(there)
        def _():
            tile_copy(mine, theirs, to_band, to_freq).start()

        @pl.when(jnp.logical_not(there))
        def _():
            tiles[mine] = jnp.zeros_like(tile)

    tiles[4] = tile[...]
    wide[:, deep : deep + cells] = spectrum[...]
    route_own[me] = route_out[me]

    @pl.when(jnp.logical_not(has_low))
    def _():
        wide[:, :deep] = jnp.zeros((DIR, deep), jnp.float32)
        route_low[...] = jnp.zeros_like(route_low)
        again[:, :near] = jnp.zeros((DIR, near), jnp.float32)

    @pl.when(jnp.logical_not(has_high))
    def _():
        wide[:, deep + cells :] = jnp.zeros((DIR, deep), jnp.float32)
        route_high[...] = jnp.zeros_like(route_high)
        again[:, near + cells :] = jnp.zeros((DIR, near), jnp.float32)

    others(lambda f: copy(
        route_out.at[f], route_own.at[f], route_sems, (f,), (f,), band, f
    ).wait_recv())

    @pl.when(has_low)
    def _():
        every(lambda f: copy(
            route_out.at[f], route_low.at[f], edge_route_sems,
            (1, f), (1, f), band - 1, f,
        ).wait_recv())
        halo_high.wait_recv()

    @pl.when(has_high)
    def _():
        every(lambda f: copy(
            route_out.at[f], route_high.at[f], edge_route_sems,
            (0, f), (0, f), band + 1, f,
        ).wait_recv())
        halo_low.wait_recv()

    tile_lanes = tile.shape[1]
    tile_cols = tile_lanes * cols // cells
    lane = lax.broadcasted_iota(jnp.int32, (2, 128), 1)
    number = me.astype(jnp.float32) + 0.5
    rate = 0.5 + 0.3 * number / freqs
    factor = (0.5 + 1.5 * number / freqs) * DIR ** (-0.5)
    column = lax.broadcasted_iota(jnp.int32, base.shape, 1)
    table[...] = base[...] * jnp.where(column < 2, rate, factor)

    def spread(ref, first_row, rows, start):
        per_block = max(128 // cols, 1)
        for block in range(rows * cols // 128):
            total = jnp.zeros((2, 128), jnp.float32)
            for j in range(freqs):
                for k in range(per_block):
                    at = block * 128 + k * cols if cols <= 128 else block * 128
                    row, col = at // cols, at % cols
                    lead = k * cols + j * tile_cols - col
                    if lead < 0 or lead >= 128:
                        continue
                    shift = (lead - (first_row + row) * tile_cols) % tile_lanes
                    piece = ref[j] if shift == 0 else pltpu.roll(ref[j], shift, 1)
                    total = jnp.where((lane >= lead) & (lane < lead + tile_cols), piece, total)
            drift[:, start + block * 128 : start + (block + 1) * 128] = 0.15 * jnp.tanh(total)

    rows = cells // cols
    spread(route_low, rows - DEEP, DEEP, 0)
    spread(route_own, 0, rows, deep)
    spread(route_high, 0, DEEP, deep + cells)
    groups = [(low, min(low + 8, DIR)) for low in range(0, DIR, 8)]

    def cycle(source_ref, cycle_index, skip, keep):
        span = source_ref.shape[1]
        window = slice(skip, skip + span)
        shape = (1, span)
        sea = masks[SUB * CYCLES : SUB * CYCLES + 1, window]
        first = masks[SUB * CYCLES + 1 : SUB * CYCLES + 2, window]
        last = masks[SUB * CYCLES + 2 : SUB * CYCLES + 3, window]
        flags = masks[SUB * cycle_index : SUB * (cycle_index + 1), window]
        drift_east, drift_north = drift[0:1, window], drift[1:2, window]
        for low, high in groups:
            state = advect(
                source_ref[low:high, :], table[low:high, :], flags, sea, first, last,
                drift_north, drift_east, cols,
            )
            keep(low, high, state)

    def send_out(index):
        def out_copy(f):
            return copy(
                leave.at[index, :, pl.ds(pl.multiple_of(f * chunk, chunk), chunk)],
                arrive.at[index, me], out_sems, (index, f), (index, me), band, f,
            )

        others(lambda f: out_copy(f).start())
        arrive[index, me] = leave[index, :, pl.ds(pl.multiple_of(me * chunk, chunk), chunk)]

    def wait_out(index):
        others(lambda f: copy(
            leave.at[index, :, pl.ds(0, chunk)], arrive.at[index, f], out_sems,
            (index, f), (index, f), band, f,
        ).wait_recv())

    def source(index):
        whole = jnp.concatenate([arrive[index, f] for f in range(freqs)], axis=0)
        gain = jnp.dot(
            gain_matrix[...], whole.astype(jnp.bfloat16), preferred_element_type=jnp.float32
        )
        quartic = jnp.dot(
            quad_matrix[...],
            (whole * whole).astype(jnp.bfloat16),
            preferred_element_type=jnp.float32,
        )
        updated = whole * (1.0 + 0.5 * jnp.tanh(gain) - 0.25 * jnp.tanh(quartic))
        for f in range(freqs):
            back[index, f] = updated[f * DIR : (f + 1) * DIR]

    def place(ref, start, number):
        return ref.at[:, pl.ds(pl.multiple_of(start + number * chunk, chunk), chunk)]

    def send_back(index, ref, start):
        others(lambda f: copy(
            back.at[index, f], place(ref, start, me), back_sems,
            (index, f), (index, me), band, f,
        ).start())
        ref[:, pl.ds(pl.multiple_of(start + me * chunk, chunk), chunk)] = back[index, me]

    def wait_back(index, ref, start):
        others(lambda f: copy(
            back.at[index, f], place(ref, start, f), back_sems,
            (index, f), (index, f), band, f,
        ).wait_recv())

    def keep_first(low, high, state):
        leave[0, low:high, :] = state[:, deep : deep + cells]
        shown = state[:, near : near + cells + 2 * (deep - near)]
        east = jnp.sum(shown * table[low:high, 2:3], axis=0, keepdims=True)
        north = jnp.sum(shown * table[low:high, 3:4], axis=0, keepdims=True)
        if low == 0:
            moments_send[0:1, :] = east
            moments_send[1:2, :] = north
        else:
            moments_send[0:1, :] += east
            moments_send[1:2, :] += north

    def keep_last(low, high, state):
        leave[1, low:high, :] = state[:, near : near + cells]

    def moment_copy(f):
        return copy(moments_send, moments.at[me], moment_sems, (f,), (me,), band, f)

    near_tiles(tile_start)
    cycle(wide, 0, 0, keep_first)
    send_out(0)
    moments[me] = moments_send[...]
    wait_out(0)
    source(0)

    def edge_low(f):
        return copy(
            back.at[0, f], place(again, near + cells, me), edge_sems,
            (0, f), (0, me), band - 1, f,
        )

    def edge_high(f):
        return copy(
            back.at[0, f], place(again, 0, me - (freqs - edges)), edge_sems,
            (1, f), (1, me), band + 1, f,
        )

    sends_low = has_low & (me < edges)
    sends_high = has_high & (me >= freqs - edges)

    @pl.when(sends_low)
    def _():
        every(lambda f: edge_low(f).start())

    @pl.when(sends_high)
    def _():
        every(lambda f: edge_high(f).start())

    send_back(0, again, near)

    def tile_wait(there, mine, theirs, to_band, to_freq):
        @pl.when(there)
        def _():
            copy(tile, tiles.at[mine], tile_sems, (mine,), (mine,), to_band, to_freq).wait_recv()

    wait_back(0, again, near)

    @pl.when(has_low)
    def _():
        for number in range(edges):
            copy(
                back.at[0, 0], place(again, 0, number), edge_sems,
                (1, 0), (1, freqs - edges + number), band - 1, freqs - edges + number,
            ).wait_recv()

    @pl.when(has_high)
    def _():
        for number in range(edges):
            copy(
                back.at[0, 0], place(again, near + cells, number), edge_sems,
                (0, 0), (0, number), band + 1, number,
            ).wait_recv()

    others(lambda f: moment_copy(f).start())
    cycle(again, 1, deep - near, keep_last)
    send_out(1)
    wait_out(1)
    source(1)
    send_back(1, final, 0)
    near_tiles(tile_wait)
    tiles_out[...] = tiles[...]
    others(lambda f: copy(
        moments_send, moments.at[f], moment_sems, (f,), (f,), band, f
    ).wait_recv())
    moments_out[...] = moments[...]

    others(lambda f: route_copy(f).wait_send())
    others(lambda f: moment_copy(f).wait_send())

    @pl.when(has_low)
    def _():
        every(lambda f: route_to_low(f).wait_send())
        halo_low.wait_send()

    @pl.when(has_high)
    def _():
        every(lambda f: route_to_high(f).wait_send())
        halo_high.wait_send()

    def tile_sent(there, mine, theirs, to_band, to_freq):
        @pl.when(there)
        def _():
            tile_copy(mine, theirs, to_band, to_freq).wait_send()

    near_tiles(tile_sent)

    @pl.when(sends_low)
    def _():
        every(lambda f: edge_low(f).wait_send())

    @pl.when(sends_high)
    def _():
        every(lambda f: edge_high(f).wait_send())

    for index in range(CYCLES):
        others(lambda f: copy(
            leave.at[index, :, pl.ds(0, chunk)], arrive.at[index, me], out_sems,
            (index, f), (index, me), band, f,
        ).wait_send())
    wait_back(1, final, 0)
    result[...] = final[...]
    others(lambda f: copy(
        back.at[0, f], place(again, near, me), back_sems, (0, f), (0, me), band, f
    ).wait_send())
    others(lambda f: copy(
        back.at[1, f], place(final, 0, me), back_sems, (1, f), (1, me), band, f
    ).wait_send())


def body(
    spectrum,
    velocity,
    gain_matrix,
    quad_matrix,
    limiter_flags,
    sea_mask,
    current_route,
    stokes_route,
):
    bands = lax.axis_size("band")
    freqs = lax.axis_size("freq")
    band = lax.axis_index("band")
    me = lax.axis_index("freq")
    rows, cols = spectrum.shape[2:]
    tile_cols = velocity.shape[3]
    cells = rows * cols
    chunk = cells // freqs
    edges = SUB * cols // chunk
    assert CYCLES == 2 and cells % freqs == 0 and chunk % 128 == 0
    assert rows >= DEEP and edges * chunk == SUB * cols and edges <= freqs
    assert rows * tile_cols == 128 and max(cols, 128) % min(cols, 128) == 0
    assert tile_cols >= OSTEPS and (EDGE * cols) % 128 == 0
    angles = (np.arange(DIR) + 0.5) * (2.0 * np.pi / DIR)
    base = np.stack([np.cos(angles), np.sin(angles)] * 2, axis=1).astype(np.float32)
    grid = jnp.concatenate([limiter_flags, sea_mask[None]], axis=0)
    grid = jnp.pad(grid, ((0, 0), (DEEP, DEEP), (0, 0)))
    grid = lax.dynamic_slice_in_dim(grid, band * rows, rows + 2 * DEEP, 1)
    at_col = jnp.broadcast_to(jnp.arange(cols), grid.shape[1:])
    sides = jnp.stack([at_col == 0, at_col == cols - 1]).astype(jnp.int32)
    masks = jnp.concatenate([grid, sides], axis=0).astype(jnp.float32)
    masks = masks.reshape(masks.shape[0], -1)
    tile_cells = rows * tile_cols
    tile = velocity.reshape(2 * LAYERS, tile_cells)
    shown = (rows + 2 * EDGE) * cols
    deep = DEEP * cols
    f32 = jnp.float32
    vmem = pl.BlockSpec(memory_space=pltpu.VMEM)
    dma = pltpu.SemaphoreType.DMA
    result, moments, tiles = pl.pallas_call(
        functools.partial(kernel, bands, freqs, cols),
        out_shape=(
            jax.ShapeDtypeStruct((DIR, cells), f32),
            jax.ShapeDtypeStruct((freqs, 2, shown), f32),
            jax.ShapeDtypeStruct((9, 2 * LAYERS, tile_cells), f32),
        ),
        in_specs=[pl.BlockSpec(memory_space=pltpu.SMEM)] + [vmem] * 6,
        out_specs=(vmem, vmem, vmem),
        scratch_shapes=[
            pltpu.VMEM((DIR, cells + 2 * deep), f32),
            pltpu.VMEM((freqs, 2, tile_cells), f32),
            pltpu.VMEM((freqs, 2, tile_cells), f32),
            pltpu.VMEM((freqs, 2, tile_cells), f32),
            pltpu.VMEM((freqs, 2, tile_cells), f32),
            pltpu.VMEM((DIR, 4), f32),
            pltpu.VMEM((CYCLES, DIR, cells), f32),
            pltpu.VMEM((CYCLES, freqs, DIR, chunk), f32),
            pltpu.VMEM((CYCLES, freqs, DIR, chunk), f32),
            pltpu.VMEM((DIR, cells + 2 * SUB * cols), f32),
            pltpu.VMEM((2, shown), f32),
            pltpu.VMEM((freqs, 2, shown), f32),
            pltpu.VMEM((9, 2 * LAYERS, tile_cells), f32),
            pltpu.VMEM((2, cells + 2 * deep), f32),
            pltpu.VMEM((DIR, cells), f32),
            dma((2, 2)),
            dma((2, freqs)),
            dma((2, 2, freqs)),
            dma((2, 9)),
            dma((2, CYCLES, freqs)),
            dma((2, freqs)),
            dma((2, CYCLES, freqs)),
            dma((2, 2, freqs)),
        ],
        compiler_params=pltpu.CompilerParams(
            collective_id=0, has_side_effects=True, vmem_limit_bytes=60 * 1024 * 1024
        ),
    )(
        current_route,
        spectrum.reshape(DIR, cells),
        tile,
        gain_matrix,
        quad_matrix,
        masks,
        jnp.asarray(base),
    )
    span = tile_cols + 2 * EDGE
    moments = moments.reshape(freqs, 2, rows + 2 * EDGE, cols)
    moments = jnp.pad(moments, ((0, 0), (0, 0), (0, 0), (EDGE, EDGE)))
    moments = lax.dynamic_slice_in_dim(moments, me * tile_cols, span, 3)
    drift = jnp.einsum(
        "fl,fsrc->slrc", deposit_table(stokes_route), moments, precision=precise
    )
    tiles = tiles.reshape(3, 3, 2, LAYERS, rows, tile_cols)
    strips = [
        jnp.concatenate(
            [tiles[0, k][:, :, rows - OSTEPS :], tiles[1, k], tiles[2, k][:, :, :OSTEPS]], axis=2
        )
        for k in range(3)
    ]
    ocean = jnp.concatenate(
        [strips[0][..., tile_cols - OSTEPS :], strips[1], strips[2][..., :OSTEPS]], axis=3
    )
    sea_wide = lax.dynamic_slice(
        jnp.pad(sea_mask, EDGE), (band * rows, me * tile_cols), (rows + 2 * EDGE, span)
    )
    for step_index in range(OSTEPS):
        high, wide = ocean.shape[2] - 2, ocean.shape[3] - 2
        trim = step_index
        ocean = ocean_step(
            ocean,
            drift[:, :, trim : trim + high, trim : trim + wide],
            sea_wide[trim : trim + high, trim : trim + wide],
        )
    return (result.reshape(1, DIR, rows, cols), ocean)


def solution(mesh):
    return jax.shard_map(
        body,
        mesh=mesh,
        in_specs=(
            P("freq", None, "band", None),
            P(None, None, "band", "freq"),
            P(),
            P(),
            P(),
            P(),
            P(),
            P(),
        ),
        out_specs=(P("freq", None, "band", None), P(None, None, "band", "freq")),
        check_vma=False,
    )
```

```python
import functools

import jax
import jax.numpy as jnp
import numpy as np
from jax import lax
from jax.experimental import pallas as pl
from jax.experimental.pallas import tpu as pltpu
from jax.sharding import PartitionSpec as P

DIR = 36
F_DEV = 1
LAYERS = 24
SUB = 4
CYCLES = 2
OSTEPS = 3


precise = lax.Precision.HIGHEST
ocean_dt = 0.2
viscous = 0.5
coriolis = 1.0
mixing = 0.5
friction = 0.1


EDGE = OSTEPS - 1
DEEP = SUB + EDGE
MESH = pl.DeviceIdType.MESH


def advect(state, table, face_flags, sea, first, last, drift_north, drift_east, cols):
    lanes = state.shape[1]
    up = lanes - cols
    rate_east, rate_north = table[:, 0:1], table[:, 1:2]
    inner = 1.0 - last

    def parts(courant):
        size = jnp.abs(courant)
        return 0.5 * courant, 0.5 * size, 0.5 * (courant * courant - size)

    north = parts(rate_north + 0.5 * (drift_north + pltpu.roll(drift_north, up, 1)))
    east = parts(rate_east + 0.5 * (drift_east + inner * pltpu.roll(drift_east, lanes - 1, 1)))
    west = parts(rate_east + 0.5 * drift_east)
    west_base = first * (west[0] - west[1])
    west_more = first * west[2]
    for step_index in range(SUB):
        flags = face_flags[step_index : step_index + 1]
        flag_north = pltpu.roll(flags, up, 1)
        flag_east = inner * pltpu.roll(flags, lanes - 1, 1)
        above = pltpu.roll(state, up, 1)
        flux = north[0] * (state + above) + (north[1] + flag_north * north[2]) * (state - above)
        state = state - (flux - pltpu.roll(flux, cols, 1))
        beside = inner * pltpu.roll(state, lanes - 1, 1)
        flux = east[0] * (state + beside) + (east[1] + flag_east * east[2]) * (state - beside)
        lower = (1.0 - first) * pltpu.roll(flux, 1, 1) + state * (west_base - flags * west_more)
        state = (state - (flux - lower)) * sea
    return state


def kernel(
    bands,
    freqs,
    cols,
    route,
    stokes_route,
    spectrum,
    tile,
    gain_matrix,
    quad_matrix,
    masks,
    base,
    result,
    ocean_out,
    ocean,
    wide,
    route_out,
    route_own,
    route_low,
    route_high,
    table,
    leave,
    arrive,
    back,
    again,
    moments_send,
    moments,
    tiles,
    drift,
    final,
    halo_sems,
    route_sems,
    edge_route_sems,
    tile_sems,
    out_sems,
    moment_sems,
    back_sems,
    edge_sems,
):
    band = lax.axis_index("band")
    me = lax.axis_index("freq")
    cells = spectrum.shape[1]
    chunk = cells // freqs
    deep = DEEP * cols
    near = SUB * cols
    edges = near // chunk
    has_low = band > 0
    has_high = band < bands - 1

    def others(fn):
        def step(i, carry):
            fn(lax.rem(me + i, freqs))
            return carry

        lax.fori_loop(1, freqs, step, 0)

    def every(fn):
        def step(i, carry):
            fn(i)
            return carry

        lax.fori_loop(0, freqs, step, 0)

    def copy(src, dst, sems, slot_send, slot_recv, to_band, to_freq):
        return pltpu.make_async_remote_copy(
            src_ref=src,
            dst_ref=dst,
            send_sem=sems.at[(0,) + slot_send],
            recv_sem=sems.at[(1,) + slot_recv],
            device_id=(to_band, to_freq),
            device_id_type=MESH,
        )

    barrier = pltpu.get_barrier_semaphore()

    def greet(to_band, to_freq):
        pl.semaphore_signal(barrier, inc=1, device_id=(to_band, to_freq), device_id_type=MESH)

    others(lambda f: greet(band, f))

    @pl.when(has_low)
    def _():
        every(lambda f: greet(band - 1, f))

    @pl.when(has_high)
    def _():
        every(lambda f: greet(band + 1, f))

    def prepare(f):
        route_out[f, 0:1, :] = tile[pl.ds(route[f], 1), :]
        route_out[f, 1:2, :] = tile[pl.ds(LAYERS + route[f], 1), :]

    every(prepare)
    count = freqs - 1 + freqs * (has_low.astype(jnp.int32) + has_high.astype(jnp.int32))
    pl.semaphore_wait(barrier, count)

    halo_low = copy(
        spectrum.at[:, pl.ds(0, deep)],
        wide.at[:, pl.ds(deep + cells, deep)],
        halo_sems,
        (0,),
        (0,),
        band - 1,
        me,
    )
    halo_high = copy(
        spectrum.at[:, pl.ds(cells - deep, deep)],
        wide.at[:, pl.ds(0, deep)],
        halo_sems,
        (1,),
        (1,),
        band + 1,
        me,
    )

    def route_copy(f):
        return copy(route_out.at[f], route_own.at[me], route_sems, (f,), (me,), band, f)

    def route_to_low(f):
        return copy(
            route_out.at[f], route_high.at[me], edge_route_sems,
            (0, f), (0, me), band - 1, f,
        )

    def route_to_high(f):
        return copy(
            route_out.at[f], route_low.at[me], edge_route_sems,
            (1, f), (1, me), band + 1, f,
        )

    others(lambda f: route_copy(f).start())

    @pl.when(has_low)
    def _():
        every(lambda f: route_to_low(f).start())
        halo_low.start()

    @pl.when(has_high)
    def _():
        every(lambda f: route_to_high(f).start())
        halo_high.start()

    def near_tiles(fn):
        for down in (-1, 0, 1):
            for side in (-1, 0, 1):
                if down == 0 and side == 0:
                    continue
                to_band, to_freq = band + down, me + side
                there = (to_band >= 0) & (to_band < bands) & (to_freq >= 0) & (to_freq < freqs)
                mine = 3 * (1 + down) + 1 + side
                fn(there, mine, 8 - mine, to_band, to_freq)

    def tile_copy(mine, theirs, to_band, to_freq):
        return copy(tile, tiles.at[theirs], tile_sems, (mine,), (theirs,), to_band, to_freq)

    def tile_start(there, mine, theirs, to_band, to_freq):
        @pl.when(there)
        def _():
            tile_copy(mine, theirs, to_band, to_freq).start()

        @pl.when(jnp.logical_not(there))
        def _():
            tiles[mine] = jnp.zeros_like(tile)

    tiles[4] = tile[...]
    wide[:, deep : deep + cells] = spectrum[...]
    route_own[me] = route_out[me]

    @pl.when(jnp.logical_not(has_low))
    def _():
        wide[:, :deep] = jnp.zeros((DIR, deep), jnp.float32)
        route_low[...] = jnp.zeros_like(route_low)
        again[:, :near] = jnp.zeros((DIR, near), jnp.float32)

    @pl.when(jnp.logical_not(has_high))
    def _():
        wide[:, deep + cells :] = jnp.zeros((DIR, deep), jnp.float32)
        route_high[...] = jnp.zeros_like(route_high)
        again[:, near + cells :] = jnp.zeros((DIR, near), jnp.float32)

    others(lambda f: copy(
        route_out.at[f], route_own.at[f], route_sems, (f,), (f,), band, f
    ).wait_recv())

    @pl.when(has_low)
    def _():
        every(lambda f: copy(
            route_out.at[f], route_low.at[f], edge_route_sems,
            (1, f), (1, f), band - 1, f,
        ).wait_recv())
        halo_high.wait_recv()

    @pl.when(has_high)
    def _():
        every(lambda f: copy(
            route_out.at[f], route_high.at[f], edge_route_sems,
            (0, f), (0, f), band + 1, f,
        ).wait_recv())
        halo_low.wait_recv()

    tile_lanes = tile.shape[1]
    tile_cols = tile_lanes * cols // cells
    lane = lax.broadcasted_iota(jnp.int32, (2, 128), 1)
    number = me.astype(jnp.float32) + 0.5
    rate = 0.5 + 0.3 * number / freqs
    factor = (0.5 + 1.5 * number / freqs) * DIR ** (-0.5)
    column = lax.broadcasted_iota(jnp.int32, base.shape, 1)
    table[...] = base[...] * jnp.where(column < 2, rate, factor)

    def spread(ref, first_row, rows, start):
        per_block = max(128 // cols, 1)
        for block in range(rows * cols // 128):
            total = jnp.zeros((2, 128), jnp.float32)
            for j in range(freqs):
                for k in range(per_block):
                    at = block * 128 + k * cols if cols <= 128 else block * 128
                    row, col = at // cols, at % cols
                    lead = k * cols + j * tile_cols - col
                    if lead < 0 or lead >= 128:
                        continue
                    shift = (lead - (first_row + row) * tile_cols) % tile_lanes
                    piece = ref[j] if shift == 0 else pltpu.roll(ref[j], shift, 1)
                    total = jnp.where((lane >= lead) & (lane < lead + tile_cols), piece, total)
            drift[:, start + block * 128 : start + (block + 1) * 128] = 0.15 * jnp.tanh(total)

    rows = cells // cols
    spread(route_low, rows - DEEP, DEEP, 0)
    spread(route_own, 0, rows, deep)
    spread(route_high, 0, DEEP, deep + cells)
    groups = [(low, min(low + 8, DIR)) for low in range(0, DIR, 8)]

    def cycle(source_ref, cycle_index, skip, keep):
        span = source_ref.shape[1]
        window = slice(skip, skip + span)
        shape = (1, span)
        sea = masks[SUB * CYCLES : SUB * CYCLES + 1, window]
        first = masks[SUB * CYCLES + 1 : SUB * CYCLES + 2, window]
        last = masks[SUB * CYCLES + 2 : SUB * CYCLES + 3, window]
        flags = masks[SUB * cycle_index : SUB * (cycle_index + 1), window]
        drift_east, drift_north = drift[0:1, window], drift[1:2, window]
        for low, high in groups:
            state = advect(
                source_ref[low:high, :], table[low:high, :], flags, sea, first, last,
                drift_north, drift_east, cols,
            )
            keep(low, high, state)

    def send_out(index):
        def out_copy(f):
            return copy(
                leave.at[index, :, pl.ds(pl.multiple_of(f * chunk, chunk), chunk)],
                arrive.at[index, me], out_sems, (index, f), (index, me), band, f,
            )

        others(lambda f: out_copy(f).start())
        arrive[index, me] = leave[index, :, pl.ds(pl.multiple_of(me * chunk, chunk), chunk)]

    def wait_out(index):
        others(lambda f: copy(
            leave.at[index, :, pl.ds(0, chunk)], arrive.at[index, f], out_sems,
            (index, f), (index, f), band, f,
        ).wait_recv())

    def source(index):
        whole = jnp.concatenate([arrive[index, f] for f in range(freqs)], axis=0)
        gain = jnp.dot(
            gain_matrix[...], whole.astype(jnp.bfloat16), preferred_element_type=jnp.float32
        )
        quartic = jnp.dot(
            quad_matrix[...],
            (whole * whole).astype(jnp.bfloat16),
            preferred_element_type=jnp.float32,
        )
        updated = whole * (1.0 + 0.5 * jnp.tanh(gain) - 0.25 * jnp.tanh(quartic))
        for f in range(freqs):
            back[index, f] = updated[f * DIR : (f + 1) * DIR]

    def place(ref, start, number):
        return ref.at[:, pl.ds(pl.multiple_of(start + number * chunk, chunk), chunk)]

    def send_back(index, ref, start):
        others(lambda f: copy(
            back.at[index, f], place(ref, start, me), back_sems,
            (index, f), (index, me), band, f,
        ).start())
        ref[:, pl.ds(pl.multiple_of(start + me * chunk, chunk), chunk)] = back[index, me]

    def wait_back(index, ref, start):
        others(lambda f: copy(
            back.at[index, f], place(ref, start, f), back_sems,
            (index, f), (index, f), band, f,
        ).wait_recv())

    high_rows = rows + 2 * OSTEPS
    pitch = 8
    while pitch < tile_cols + 2 * OSTEPS:
        pitch *= 2
    per = 128 // pitch
    blocks = -(-high_rows // per)
    ocean_lanes = blocks * 128

    def assemble_ocean():
        at = lax.broadcasted_iota(jnp.int32, tile.shape, 1)
        for block in range(blocks):
            total = jnp.zeros(tile.shape, jnp.float32)
            for row in range(block * per, min((block + 1) * per, high_rows)):
                down = 0 if row < OSTEPS else (1 if row < OSTEPS + rows else 2)
                from_row = row - OSTEPS + rows * (1 - down)
                lead = (row % per) * pitch
                for side, width, from_col in (
                    (0, OSTEPS, tile_cols - OSTEPS),
                    (1, tile_cols, 0),
                    (2, OSTEPS, 0),
                ):
                    shift = (lead - from_row * tile_cols - from_col) % 128
                    piece = tiles[3 * down + side]
                    piece = piece if shift == 0 else pltpu.roll(piece, shift, 1)
                    total = jnp.where((at >= lead) & (at < lead + width), piece, total)
                    lead += width
            ocean[:, block * 128 : (block + 1) * 128] = total

    def window(load, limit, skip, first, count, pad, like):
        at = lax.broadcasted_iota(jnp.int32, like, 1)
        width = tile_cols + 2 * pad
        outs = []
        for block in range(blocks):
            total = jnp.zeros(like, jnp.float32)
            for row in range(max(block * per, first), min((block + 1) * per, first + count)):
                lead = (row % per) * pitch + OSTEPS - pad
                start = (row - first + skip) * cols + me * tile_cols - pad + 128
                number, offset = start // 128 - 1, start % 128
                shift = (lead + 128 - offset) % 128
                left = pltpu.roll(load(jnp.maximum(number, 0)), shift, 1)
                right = pltpu.roll(load(jnp.minimum(number + 1, limit - 1)), shift, 1)
                piece = jnp.where(at < lead + 128 - offset, left, right)
                total = jnp.where((at >= lead) & (at < lead + width), piece, total)
            outs.append(total)
        return jnp.concatenate(outs, axis=1)

    def run_ocean():
        layer = lax.broadcasted_iota(jnp.int32, (LAYERS, 1), 0)
        shown_blocks = moments.shape[2] // 128
        zero = jnp.zeros((LAYERS, ocean_lanes), jnp.float32)

        def gather(g, carry):
            def load(number):
                return moments[g, :, pl.ds(pl.multiple_of(number * 128, 128), 128)]

            part = window(load, shown_blocks, 0, OSTEPS - EDGE, rows + 2 * EDGE, EDGE, (2, 128))
            deposit = jnp.zeros((LAYERS, 1), jnp.float32)
            for j in range(stokes_route.shape[1]):
                hit = (layer == stokes_route[g, j]).astype(jnp.float32)
                deposit = deposit + hit * (1.0 / (1.0 + j))
            return (carry[0] + deposit * part[0:1], carry[1] + deposit * part[1:2])

        east, north = lax.fori_loop(0, freqs, gather, (zero, zero))

        def load_sea(number):
            at = pl.ds(pl.multiple_of(number * 128, 128), 128)
            return masks[SUB * CYCLES : SUB * CYCLES + 1, at]

        sea = window(
            load_sea, masks.shape[1] // 128, DEEP - OSTEPS, 0, high_rows, OSTEPS, (1, 128)
        )
        at = lax.broadcasted_iota(jnp.int32, (1, ocean_lanes), 1)
        col = me * tile_cols + (at & (pitch - 1)) - OSTEPS
        sea = jnp.where((col >= 0) & (col < cols), sea, 0.0)
        level = lax.broadcasted_iota(jnp.int32, (LAYERS, ocean_lanes), 0)
        u, v = ocean[:LAYERS, :], ocean[LAYERS:, :]

        def spreading(field):
            sides = pltpu.roll(field, 1, 1) + pltpu.roll(field, ocean_lanes - 1, 1)
            rows_by = pltpu.roll(field, pitch, 1) + pltpu.roll(field, ocean_lanes - pitch, 1)
            over = jnp.where(level < LAYERS - 1, pltpu.roll(field, LAYERS - 1, 0), 0.0)
            under = jnp.where(level > 0, pltpu.roll(field, 1, 0), 0.0)
            return (
                viscous * (sides + rows_by - 4.0 * field)
                + mixing * (over + under - 2.0 * field)
                - friction * field
            )

        for step_index in range(OSTEPS):
            u, v = (
                (u + ocean_dt * (spreading(u) + coriolis * (v + north))) * sea,
                (v + ocean_dt * (spreading(v) - coriolis * (u + east))) * sea,
            )
        both = jnp.concatenate([u, v], axis=0)
        at = lax.broadcasted_iota(jnp.int32, tile.shape, 1)
        total = jnp.zeros(tile.shape, jnp.float32)
        for row in range(rows):
            block, slot = (row + OSTEPS) // per, (row + OSTEPS) % per
            lead = row * tile_cols
            shift = (lead - slot * pitch - OSTEPS) % 128
            piece = both[:, block * 128 : (block + 1) * 128]
            piece = piece if shift == 0 else pltpu.roll(piece, shift, 1)
            total = jnp.where((at >= lead) & (at < lead + tile_cols), piece, total)
        ocean_out[...] = total

    def keep_first(low, high, state):
        leave[0, low:high, :] = state[:, deep : deep + cells]
        shown = state[:, near : near + cells + 2 * (deep - near)]
        east = jnp.sum(shown * table[low:high, 2:3], axis=0, keepdims=True)
        north = jnp.sum(shown * table[low:high, 3:4], axis=0, keepdims=True)
        if low == 0:
            moments_send[0:1, :] = east
            moments_send[1:2, :] = north
        else:
            moments_send[0:1, :] += east
            moments_send[1:2, :] += north

    def keep_last(low, high, state):
        leave[1, low:high, :] = state[:, near : near + cells]

    def moment_copy(f):
        return copy(moments_send, moments.at[me], moment_sems, (f,), (me,), band, f)

    near_tiles(tile_start)
    cycle(wide, 0, 0, keep_first)
    send_out(0)
    moments[me] = moments_send[...]
    wait_out(0)
    source(0)

    def edge_low(f):
        return copy(
            back.at[0, f], place(again, near + cells, me), edge_sems,
            (0, f), (0, me), band - 1, f,
        )

    def edge_high(f):
        return copy(
            back.at[0, f], place(again, 0, me - (freqs - edges)), edge_sems,
            (1, f), (1, me), band + 1, f,
        )

    sends_low = has_low & (me < edges)
    sends_high = has_high & (me >= freqs - edges)

    @pl.when(sends_low)
    def _():
        every(lambda f: edge_low(f).start())

    @pl.when(sends_high)
    def _():
        every(lambda f: edge_high(f).start())

    send_back(0, again, near)

    def tile_wait(there, mine, theirs, to_band, to_freq):
        @pl.when(there)
        def _():
            copy(tile, tiles.at[mine], tile_sems, (mine,), (mine,), to_band, to_freq).wait_recv()

    near_tiles(tile_wait)
    assemble_ocean()
    wait_back(0, again, near)

    @pl.when(has_low)
    def _():
        for number in range(edges):
            copy(
                back.at[0, 0], place(again, 0, number), edge_sems,
                (1, 0), (1, freqs - edges + number), band - 1, freqs - edges + number,
            ).wait_recv()

    @pl.when(has_high)
    def _():
        for number in range(edges):
            copy(
                back.at[0, 0], place(again, near + cells, number), edge_sems,
                (0, 0), (0, number), band + 1, number,
            ).wait_recv()

    others(lambda f: moment_copy(f).start())
    cycle(again, 1, deep - near, keep_last)
    send_out(1)
    others(lambda f: copy(
        moments_send, moments.at[f], moment_sems, (f,), (f,), band, f
    ).wait_recv())
    run_ocean()
    wait_out(1)
    source(1)
    send_back(1, final, 0)

    others(lambda f: route_copy(f).wait_send())
    others(lambda f: moment_copy(f).wait_send())

    @pl.when(has_low)
    def _():
        every(lambda f: route_to_low(f).wait_send())
        halo_low.wait_send()

    @pl.when(has_high)
    def _():
        every(lambda f: route_to_high(f).wait_send())
        halo_high.wait_send()

    def tile_sent(there, mine, theirs, to_band, to_freq):
        @pl.when(there)
        def _():
            tile_copy(mine, theirs, to_band, to_freq).wait_send()

    near_tiles(tile_sent)

    @pl.when(sends_low)
    def _():
        every(lambda f: edge_low(f).wait_send())

    @pl.when(sends_high)
    def _():
        every(lambda f: edge_high(f).wait_send())

    for index in range(CYCLES):
        others(lambda f: copy(
            leave.at[index, :, pl.ds(0, chunk)], arrive.at[index, me], out_sems,
            (index, f), (index, me), band, f,
        ).wait_send())
    wait_back(1, final, 0)
    result[...] = final[...]
    others(lambda f: copy(
        back.at[0, f], place(again, near, me), back_sems, (0, f), (0, me), band, f
    ).wait_send())
    others(lambda f: copy(
        back.at[1, f], place(final, 0, me), back_sems, (1, f), (1, me), band, f
    ).wait_send())


def body(
    spectrum,
    velocity,
    gain_matrix,
    quad_matrix,
    limiter_flags,
    sea_mask,
    current_route,
    stokes_route,
):
    bands = lax.axis_size("band")
    freqs = lax.axis_size("freq")
    band = lax.axis_index("band")
    me = lax.axis_index("freq")
    rows, cols = spectrum.shape[2:]
    tile_cols = velocity.shape[3]
    cells = rows * cols
    chunk = cells // freqs
    edges = SUB * cols // chunk
    assert CYCLES == 2 and cells % freqs == 0 and chunk % 128 == 0
    assert rows >= DEEP and edges * chunk == SUB * cols and edges <= freqs
    assert rows * tile_cols == 128 and max(cols, 128) % min(cols, 128) == 0
    assert tile_cols >= OSTEPS and (EDGE * cols) % 128 == 0
    angles = (np.arange(DIR) + 0.5) * (2.0 * np.pi / DIR)
    base = np.stack([np.cos(angles), np.sin(angles)] * 2, axis=1).astype(np.float32)
    grid = jnp.concatenate([limiter_flags, sea_mask[None]], axis=0)
    grid = jnp.pad(grid, ((0, 0), (DEEP, DEEP), (0, 0)))
    grid = lax.dynamic_slice_in_dim(grid, band * rows, rows + 2 * DEEP, 1)
    at_col = jnp.broadcast_to(jnp.arange(cols), grid.shape[1:])
    sides = jnp.stack([at_col == 0, at_col == cols - 1]).astype(jnp.int32)
    masks = jnp.concatenate([grid, sides], axis=0).astype(jnp.float32)
    masks = masks.reshape(masks.shape[0], -1)
    tile_cells = rows * tile_cols
    tile = velocity.reshape(2 * LAYERS, tile_cells)
    shown = (rows + 2 * EDGE) * cols
    deep = DEEP * cols
    f32 = jnp.float32
    vmem = pl.BlockSpec(memory_space=pltpu.VMEM)
    dma = pltpu.SemaphoreType.DMA
    pitch = 8
    while pitch < tile_cols + 2 * OSTEPS:
        pitch *= 2
    ocean_lanes = -(-(rows + 2 * OSTEPS) * pitch // 128) * 128
    result, ocean = pl.pallas_call(
        functools.partial(kernel, bands, freqs, cols),
        out_shape=(
            jax.ShapeDtypeStruct((DIR, cells), f32),
            jax.ShapeDtypeStruct((2 * LAYERS, tile_cells), f32),
        ),
        in_specs=[pl.BlockSpec(memory_space=pltpu.SMEM)] * 2 + [vmem] * 6,
        out_specs=(vmem, vmem),
        scratch_shapes=[
            pltpu.VMEM((2 * LAYERS, ocean_lanes), f32),
            pltpu.VMEM((DIR, cells + 2 * deep), f32),
            pltpu.VMEM((freqs, 2, tile_cells), f32),
            pltpu.VMEM((freqs, 2, tile_cells), f32),
            pltpu.VMEM((freqs, 2, tile_cells), f32),
            pltpu.VMEM((freqs, 2, tile_cells), f32),
            pltpu.VMEM((DIR, 4), f32),
            pltpu.VMEM((CYCLES, DIR, cells), f32),
            pltpu.VMEM((CYCLES, freqs, DIR, chunk), f32),
            pltpu.VMEM((CYCLES, freqs, DIR, chunk), f32),
            pltpu.VMEM((DIR, cells + 2 * SUB * cols), f32),
            pltpu.VMEM((2, shown), f32),
            pltpu.VMEM((freqs, 2, shown), f32),
            pltpu.VMEM((9, 2 * LAYERS, tile_cells), f32),
            pltpu.VMEM((2, cells + 2 * deep), f32),
            pltpu.VMEM((DIR, cells), f32),
            dma((2, 2)),
            dma((2, freqs)),
            dma((2, 2, freqs)),
            dma((2, 9)),
            dma((2, CYCLES, freqs)),
            dma((2, freqs)),
            dma((2, CYCLES, freqs)),
            dma((2, 2, freqs)),
        ],
        compiler_params=pltpu.CompilerParams(
            collective_id=0, has_side_effects=True, vmem_limit_bytes=60 * 1024 * 1024
        ),
    )(
        current_route,
        stokes_route,
        spectrum.reshape(DIR, cells),
        tile,
        gain_matrix,
        quad_matrix,
        masks,
        jnp.asarray(base),
    )
    return (result.reshape(1, DIR, rows, cols), ocean.reshape(velocity.shape))


def solution(mesh):
    return jax.shard_map(
        body,
        mesh=mesh,
        in_specs=(
            P("freq", None, "band", None),
            P(None, None, "band", "freq"),
            P(),
            P(),
            P(),
            P(),
            P(),
            P(),
        ),
        out_specs=(P("freq", None, "band", None), P(None, None, "band", "freq")),
        check_vma=False,
    )
```

```python
import functools

import jax
import jax.numpy as jnp
import numpy as np
from jax import lax
from jax.experimental import pallas as pl
from jax.experimental.pallas import tpu as pltpu
from jax.sharding import PartitionSpec as P

DIR = 36
F_DEV = 1
LAYERS = 24
SUB = 4
CYCLES = 2
OSTEPS = 3


precise = lax.Precision.HIGHEST
ocean_dt = 0.2
viscous = 0.5
coriolis = 1.0
mixing = 0.5
friction = 0.1


EDGE = OSTEPS - 1
DEEP = SUB + EDGE
MESH = pl.DeviceIdType.MESH


def advect(state, table, face_flags, sea, first, last, drift_north, drift_east, cols):
    lanes = state.shape[1]
    up = lanes - cols
    rate_east, rate_north = table[:, 0:1], table[:, 1:2]
    inner = 1.0 - last

    def parts(courant):
        size = jnp.abs(courant)
        return 0.5 * courant, 0.5 * size, 0.5 * (courant * courant - size)

    north = parts(rate_north + 0.5 * (drift_north + pltpu.roll(drift_north, up, 1)))
    east = parts(rate_east + 0.5 * (drift_east + inner * pltpu.roll(drift_east, lanes - 1, 1)))
    west = parts(rate_east + 0.5 * drift_east)
    west_base = first * (west[0] - west[1])
    west_more = first * west[2]
    for step_index in range(SUB):
        flags = face_flags[step_index : step_index + 1]
        flag_north = pltpu.roll(flags, up, 1)
        flag_east = inner * pltpu.roll(flags, lanes - 1, 1)
        above = pltpu.roll(state, up, 1)
        flux = north[0] * (state + above) + (north[1] + flag_north * north[2]) * (state - above)
        state = state - (flux - pltpu.roll(flux, cols, 1))
        beside = inner * pltpu.roll(state, lanes - 1, 1)
        flux = east[0] * (state + beside) + (east[1] + flag_east * east[2]) * (state - beside)
        lower = (1.0 - first) * pltpu.roll(flux, 1, 1) + state * (west_base - flags * west_more)
        state = (state - (flux - lower)) * sea
    return state


def kernel(
    bands,
    freqs,
    cols,
    route,
    stokes_route,
    spectrum,
    tile,
    gain_matrix,
    quad_matrix,
    masks,
    base,
    result,
    ocean_out,
    ocean,
    wide,
    route_out,
    route_own,
    route_low,
    route_high,
    table,
    leave,
    arrive,
    back,
    again,
    moments_send,
    moments,
    tiles,
    drift,
    final,
    halo_sems,
    route_sems,
    edge_route_sems,
    tile_sems,
    out_sems,
    moment_sems,
    back_sems,
    edge_sems,
):
    band = lax.axis_index("band")
    me = lax.axis_index("freq")
    cells = spectrum.shape[1]
    chunk = cells // freqs
    deep = DEEP * cols
    near = SUB * cols
    edges = near // chunk
    has_low = band > 0
    has_high = band < bands - 1

    def others(fn):
        def step(i, carry):
            fn(lax.rem(me + i, freqs))
            return carry

        lax.fori_loop(1, freqs, step, 0)

    def every(fn):
        def step(i, carry):
            fn(i)
            return carry

        lax.fori_loop(0, freqs, step, 0)

    def copy(src, dst, sems, slot_send, slot_recv, to_band, to_freq):
        return pltpu.make_async_remote_copy(
            src_ref=src,
            dst_ref=dst,
            send_sem=sems.at[(0,) + slot_send],
            recv_sem=sems.at[(1,) + slot_recv],
            device_id=(to_band, to_freq),
            device_id_type=MESH,
        )

    barrier = pltpu.get_barrier_semaphore()

    def greet(to_band, to_freq):
        pl.semaphore_signal(barrier, inc=1, device_id=(to_band, to_freq), device_id_type=MESH)

    others(lambda f: greet(band, f))

    @pl.when(has_low)
    def _():
        every(lambda f: greet(band - 1, f))

    @pl.when(has_high)
    def _():
        every(lambda f: greet(band + 1, f))

    def prepare(f):
        route_out[f, 0:1, :] = tile[pl.ds(route[f], 1), :]
        route_out[f, 1:2, :] = tile[pl.ds(LAYERS + route[f], 1), :]

    every(prepare)
    count = freqs - 1 + freqs * (has_low.astype(jnp.int32) + has_high.astype(jnp.int32))
    pl.semaphore_wait(barrier, count)

    halo_low = copy(
        spectrum.at[:, pl.ds(0, deep)],
        wide.at[:, pl.ds(deep + cells, deep)],
        halo_sems,
        (0,),
        (0,),
        band - 1,
        me,
    )
    halo_high = copy(
        spectrum.at[:, pl.ds(cells - deep, deep)],
        wide.at[:, pl.ds(0, deep)],
        halo_sems,
        (1,),
        (1,),
        band + 1,
        me,
    )

    def route_copy(f):
        return copy(route_out.at[f], route_own.at[me], route_sems, (f,), (me,), band, f)

    def route_to_low(f):
        return copy(
            route_out.at[f], route_high.at[me], edge_route_sems,
            (0, f), (0, me), band - 1, f,
        )

    def route_to_high(f):
        return copy(
            route_out.at[f], route_low.at[me], edge_route_sems,
            (1, f), (1, me), band + 1, f,
        )

    others(lambda f: route_copy(f).start())

    @pl.when(has_low)
    def _():
        every(lambda f: route_to_low(f).start())
        halo_low.start()

    @pl.when(has_high)
    def _():
        every(lambda f: route_to_high(f).start())
        halo_high.start()

    def near_tiles(fn):
        for down in (-1, 0, 1):
            for side in (-1, 0, 1):
                if down == 0 and side == 0:
                    continue
                to_band, to_freq = band + down, me + side
                there = (to_band >= 0) & (to_band < bands) & (to_freq >= 0) & (to_freq < freqs)
                mine = 3 * (1 + down) + 1 + side
                fn(there, mine, 8 - mine, to_band, to_freq)

    def tile_copy(mine, theirs, to_band, to_freq):
        return copy(tile, tiles.at[theirs], tile_sems, (mine,), (theirs,), to_band, to_freq)

    def tile_start(there, mine, theirs, to_band, to_freq):
        @pl.when(there)
        def _():
            tile_copy(mine, theirs, to_band, to_freq).start()

        @pl.when(jnp.logical_not(there))
        def _():
            tiles[mine] = jnp.zeros_like(tile)

    tiles[4] = tile[...]
    wide[:, deep : deep + cells] = spectrum[...]
    route_own[me] = route_out[me]

    @pl.when(jnp.logical_not(has_low))
    def _():
        wide[:, :deep] = jnp.zeros((DIR, deep), jnp.float32)
        route_low[...] = jnp.zeros_like(route_low)
        again[:, :near] = jnp.zeros((DIR, near), jnp.float32)

    @pl.when(jnp.logical_not(has_high))
    def _():
        wide[:, deep + cells :] = jnp.zeros((DIR, deep), jnp.float32)
        route_high[...] = jnp.zeros_like(route_high)
        again[:, near + cells :] = jnp.zeros((DIR, near), jnp.float32)

    others(lambda f: copy(
        route_out.at[f], route_own.at[f], route_sems, (f,), (f,), band, f
    ).wait_recv())

    @pl.when(has_low)
    def _():
        every(lambda f: copy(
            route_out.at[f], route_low.at[f], edge_route_sems,
            (1, f), (1, f), band - 1, f,
        ).wait_recv())
        halo_high.wait_recv()

    @pl.when(has_high)
    def _():
        every(lambda f: copy(
            route_out.at[f], route_high.at[f], edge_route_sems,
            (0, f), (0, f), band + 1, f,
        ).wait_recv())
        halo_low.wait_recv()

    tile_lanes = tile.shape[1]
    tile_cols = tile_lanes * cols // cells
    lane = lax.broadcasted_iota(jnp.int32, (2, 128), 1)
    number = me.astype(jnp.float32) + 0.5
    rate = 0.5 + 0.3 * number / freqs
    factor = (0.5 + 1.5 * number / freqs) * DIR ** (-0.5)
    column = lax.broadcasted_iota(jnp.int32, base.shape, 1)
    table[...] = base[...] * jnp.where(column < 2, rate, factor)

    def spread(ref, first_row, rows, start):
        per_block = max(128 // cols, 1)
        for block in range(rows * cols // 128):
            total = jnp.zeros((2, 128), jnp.float32)
            for j in range(freqs):
                for k in range(per_block):
                    at = block * 128 + k * cols if cols <= 128 else block * 128
                    row, col = at // cols, at % cols
                    lead = k * cols + j * tile_cols - col
                    if lead < 0 or lead >= 128:
                        continue
                    shift = (lead - (first_row + row) * tile_cols) % tile_lanes
                    piece = ref[j] if shift == 0 else pltpu.roll(ref[j], shift, 1)
                    total = jnp.where((lane >= lead) & (lane < lead + tile_cols), piece, total)
            drift[:, start + block * 128 : start + (block + 1) * 128] = 0.15 * jnp.tanh(total)

    rows = cells // cols
    spread(route_low, rows - DEEP, DEEP, 0)
    spread(route_own, 0, rows, deep)
    spread(route_high, 0, DEEP, deep + cells)
    groups = [(low, min(low + 8, DIR)) for low in range(0, DIR, 8)]

    def cycle(source_ref, cycle_index, skip, keep):
        span = source_ref.shape[1]
        window = slice(skip, skip + span)
        shape = (1, span)
        sea = masks[SUB * CYCLES : SUB * CYCLES + 1, window]
        first = masks[SUB * CYCLES + 1 : SUB * CYCLES + 2, window]
        last = masks[SUB * CYCLES + 2 : SUB * CYCLES + 3, window]
        flags = masks[SUB * cycle_index : SUB * (cycle_index + 1), window]
        drift_east, drift_north = drift[0:1, window], drift[1:2, window]
        for low, high in groups:
            state = advect(
                source_ref[low:high, :], table[low:high, :], flags, sea, first, last,
                drift_north, drift_east, cols,
            )
            keep(low, high, state)

    def send_out(index):
        def out_copy(f):
            return copy(
                leave.at[index, :, pl.ds(pl.multiple_of(f * chunk, chunk), chunk)],
                arrive.at[index, me], out_sems, (index, f), (index, me), band, f,
            )

        others(lambda f: out_copy(f).start())
        arrive[index, me] = leave[index, :, pl.ds(pl.multiple_of(me * chunk, chunk), chunk)]

    def wait_out(index):
        others(lambda f: copy(
            leave.at[index, :, pl.ds(0, chunk)], arrive.at[index, f], out_sems,
            (index, f), (index, f), band, f,
        ).wait_recv())

    def source(index):
        whole = jnp.concatenate([arrive[index, f] for f in range(freqs)], axis=0)
        gain = jnp.dot(
            gain_matrix[...], whole.astype(jnp.bfloat16), preferred_element_type=jnp.float32
        )
        quartic = jnp.dot(
            quad_matrix[...],
            (whole * whole).astype(jnp.bfloat16),
            preferred_element_type=jnp.float32,
        )
        updated = whole * (1.0 + 0.5 * jnp.tanh(gain) - 0.25 * jnp.tanh(quartic))
        for f in range(freqs):
            back[index, f] = updated[f * DIR : (f + 1) * DIR]

    def place(ref, start, number):
        return ref.at[:, pl.ds(pl.multiple_of(start + number * chunk, chunk), chunk)]

    def send_back(index, ref, start):
        others(lambda f: copy(
            back.at[index, f], place(ref, start, me), back_sems,
            (index, f), (index, me), band, f,
        ).start())
        ref[:, pl.ds(pl.multiple_of(start + me * chunk, chunk), chunk)] = back[index, me]

    def wait_back(index, ref, start):
        others(lambda f: copy(
            back.at[index, f], place(ref, start, f), back_sems,
            (index, f), (index, f), band, f,
        ).wait_recv())

    high_rows = rows + 2 * OSTEPS
    pitch = 8
    while pitch < tile_cols + 2 * OSTEPS:
        pitch *= 2
    per = 128 // pitch
    blocks = -(-high_rows // per)
    ocean_lanes = blocks * 128

    def assemble_ocean():
        at = lax.broadcasted_iota(jnp.int32, tile.shape, 1)
        for block in range(blocks):
            total = jnp.zeros(tile.shape, jnp.float32)
            for row in range(block * per, min((block + 1) * per, high_rows)):
                down = 0 if row < OSTEPS else (1 if row < OSTEPS + rows else 2)
                from_row = row - OSTEPS + rows * (1 - down)
                lead = (row % per) * pitch
                for side, width, from_col in (
                    (0, OSTEPS, tile_cols - OSTEPS),
                    (1, tile_cols, 0),
                    (2, OSTEPS, 0),
                ):
                    shift = (lead - from_row * tile_cols - from_col) % 128
                    piece = tiles[3 * down + side]
                    piece = piece if shift == 0 else pltpu.roll(piece, shift, 1)
                    total = jnp.where((at >= lead) & (at < lead + width), piece, total)
                    lead += width
            ocean[:, block * 128 : (block + 1) * 128] = total

    def window(load, limit, skip, first, count, pad, like):
        at = lax.broadcasted_iota(jnp.int32, like, 1)
        width = tile_cols + 2 * pad
        outs = []
        for block in range(blocks):
            total = jnp.zeros(like, jnp.float32)
            for row in range(max(block * per, first), min((block + 1) * per, first + count)):
                lead = (row % per) * pitch + OSTEPS - pad
                start = (row - first + skip) * cols + me * tile_cols - pad + 128
                number, offset = start // 128 - 1, start % 128
                shift = (lead + 128 - offset) % 128
                left = pltpu.roll(load(jnp.maximum(number, 0)), shift, 1)
                right = pltpu.roll(load(jnp.minimum(number + 1, limit - 1)), shift, 1)
                piece = jnp.where(at < lead + 128 - offset, left, right)
                total = jnp.where((at >= lead) & (at < lead + width), piece, total)
            outs.append(total)
        return jnp.concatenate(outs, axis=1)

    def gather_drift():
        layer = lax.broadcasted_iota(jnp.int32, (LAYERS, 1), 0)
        shown_blocks = moments.shape[2] // 128
        zero = jnp.zeros((LAYERS, ocean_lanes), jnp.float32)

        def gather(g, carry):
            def load(number):
                return moments[g, :, pl.ds(pl.multiple_of(number * 128, 128), 128)]

            part = window(load, shown_blocks, 0, OSTEPS - EDGE, rows + 2 * EDGE, EDGE, (2, 128))
            deposit = jnp.zeros((LAYERS, 1), jnp.float32)
            for j in range(stokes_route.shape[1]):
                hit = (layer == stokes_route[g, j]).astype(jnp.float32)
                deposit = deposit + hit * (1.0 / (1.0 + j))
            return (carry[0] + deposit * part[0:1], carry[1] + deposit * part[1:2])

        east, north = lax.fori_loop(0, freqs, gather, (zero, zero))

        def load_sea(number):
            at = pl.ds(pl.multiple_of(number * 128, 128), 128)
            return masks[SUB * CYCLES : SUB * CYCLES + 1, at]

        sea = window(
            load_sea, masks.shape[1] // 128, DEEP - OSTEPS, 0, high_rows, OSTEPS, (1, 128)
        )
        at = lax.broadcasted_iota(jnp.int32, (1, ocean_lanes), 1)
        col = me * tile_cols + (at & (pitch - 1)) - OSTEPS
        sea = jnp.where((col >= 0) & (col < cols), sea, 0.0)
        return east, north, sea

    def run_ocean(east, north, sea):
        level = lax.broadcasted_iota(jnp.int32, (LAYERS, ocean_lanes), 0)
        u, v = ocean[:LAYERS, :], ocean[LAYERS:, :]

        def spreading(field):
            sides = pltpu.roll(field, 1, 1) + pltpu.roll(field, ocean_lanes - 1, 1)
            rows_by = pltpu.roll(field, pitch, 1) + pltpu.roll(field, ocean_lanes - pitch, 1)
            over = jnp.where(level < LAYERS - 1, pltpu.roll(field, LAYERS - 1, 0), 0.0)
            under = jnp.where(level > 0, pltpu.roll(field, 1, 0), 0.0)
            return (
                viscous * (sides + rows_by - 4.0 * field)
                + mixing * (over + under - 2.0 * field)
                - friction * field
            )

        for step_index in range(OSTEPS):
            u, v = (
                (u + ocean_dt * (spreading(u) + coriolis * (v + north))) * sea,
                (v + ocean_dt * (spreading(v) - coriolis * (u + east))) * sea,
            )
        both = jnp.concatenate([u, v], axis=0)
        at = lax.broadcasted_iota(jnp.int32, tile.shape, 1)
        total = jnp.zeros(tile.shape, jnp.float32)
        for row in range(rows):
            block, slot = (row + OSTEPS) // per, (row + OSTEPS) % per
            lead = row * tile_cols
            shift = (lead - slot * pitch - OSTEPS) % 128
            piece = both[:, block * 128 : (block + 1) * 128]
            piece = piece if shift == 0 else pltpu.roll(piece, shift, 1)
            total = jnp.where((at >= lead) & (at < lead + tile_cols), piece, total)
        ocean_out[...] = total

    def keep_first(low, high, state):
        leave[0, low:high, :] = state[:, deep : deep + cells]
        shown = state[:, near : near + cells + 2 * (deep - near)]
        east = jnp.sum(shown * table[low:high, 2:3], axis=0, keepdims=True)
        north = jnp.sum(shown * table[low:high, 3:4], axis=0, keepdims=True)
        if low == 0:
            moments_send[0:1, :] = east
            moments_send[1:2, :] = north
        else:
            moments_send[0:1, :] += east
            moments_send[1:2, :] += north

    def keep_last(low, high, state):
        leave[1, low:high, :] = state[:, near : near + cells]

    def moment_copy(f):
        return copy(moments_send, moments.at[me], moment_sems, (f,), (me,), band, f)

    near_tiles(tile_start)
    cycle(wide, 0, 0, keep_first)
    send_out(0)
    moments[me] = moments_send[...]
    wait_out(0)
    source(0)

    def edge_low(f):
        return copy(
            back.at[0, f], place(again, near + cells, me), edge_sems,
            (0, f), (0, me), band - 1, f,
        )

    def edge_high(f):
        return copy(
            back.at[0, f], place(again, 0, me - (freqs - edges)), edge_sems,
            (1, f), (1, me), band + 1, f,
        )

    sends_low = has_low & (me < edges)
    sends_high = has_high & (me >= freqs - edges)

    @pl.when(sends_low)
    def _():
        every(lambda f: edge_low(f).start())

    @pl.when(sends_high)
    def _():
        every(lambda f: edge_high(f).start())

    send_back(0, again, near)

    def tile_wait(there, mine, theirs, to_band, to_freq):
        @pl.when(there)
        def _():
            copy(tile, tiles.at[mine], tile_sems, (mine,), (mine,), to_band, to_freq).wait_recv()

    near_tiles(tile_wait)
    assemble_ocean()
    wait_back(0, again, near)

    @pl.when(has_low)
    def _():
        for number in range(edges):
            copy(
                back.at[0, 0], place(again, 0, number), edge_sems,
                (1, 0), (1, freqs - edges + number), band - 1, freqs - edges + number,
            ).wait_recv()

    @pl.when(has_high)
    def _():
        for number in range(edges):
            copy(
                back.at[0, 0], place(again, near + cells, number), edge_sems,
                (0, 0), (0, number), band + 1, number,
            ).wait_recv()

    others(lambda f: moment_copy(f).start())
    cycle(again, 1, deep - near, keep_last)
    send_out(1)
    others(lambda f: copy(
        moments_send, moments.at[f], moment_sems, (f,), (f,), band, f
    ).wait_recv())
    drifts = gather_drift()
    wait_out(1)
    source(1)
    send_back(1, final, 0)
    run_ocean(*drifts)

    others(lambda f: route_copy(f).wait_send())
    others(lambda f: moment_copy(f).wait_send())

    @pl.when(has_low)
    def _():
        every(lambda f: route_to_low(f).wait_send())
        halo_low.wait_send()

    @pl.when(has_high)
    def _():
        every(lambda f: route_to_high(f).wait_send())
        halo_high.wait_send()

    def tile_sent(there, mine, theirs, to_band, to_freq):
        @pl.when(there)
        def _():
            tile_copy(mine, theirs, to_band, to_freq).wait_send()

    near_tiles(tile_sent)

    @pl.when(sends_low)
    def _():
        every(lambda f: edge_low(f).wait_send())

    @pl.when(sends_high)
    def _():
        every(lambda f: edge_high(f).wait_send())

    for index in range(CYCLES):
        others(lambda f: copy(
            leave.at[index, :, pl.ds(0, chunk)], arrive.at[index, me], out_sems,
            (index, f), (index, me), band, f,
        ).wait_send())
    wait_back(1, final, 0)
    result[...] = final[...]
    others(lambda f: copy(
        back.at[0, f], place(again, near, me), back_sems, (0, f), (0, me), band, f
    ).wait_send())
    others(lambda f: copy(
        back.at[1, f], place(final, 0, me), back_sems, (1, f), (1, me), band, f
    ).wait_send())


def body(
    spectrum,
    velocity,
    gain_matrix,
    quad_matrix,
    limiter_flags,
    sea_mask,
    current_route,
    stokes_route,
):
    bands = lax.axis_size("band")
    freqs = lax.axis_size("freq")
    band = lax.axis_index("band")
    me = lax.axis_index("freq")
    rows, cols = spectrum.shape[2:]
    tile_cols = velocity.shape[3]
    cells = rows * cols
    chunk = cells // freqs
    edges = SUB * cols // chunk
    assert CYCLES == 2 and cells % freqs == 0 and chunk % 128 == 0
    assert rows >= DEEP and edges * chunk == SUB * cols and edges <= freqs
    assert rows * tile_cols == 128 and max(cols, 128) % min(cols, 128) == 0
    assert tile_cols >= OSTEPS and (EDGE * cols) % 128 == 0
    angles = (np.arange(DIR) + 0.5) * (2.0 * np.pi / DIR)
    base = np.stack([np.cos(angles), np.sin(angles)] * 2, axis=1).astype(np.float32)
    grid = jnp.concatenate([limiter_flags, sea_mask[None]], axis=0)
    grid = jnp.pad(grid, ((0, 0), (DEEP, DEEP), (0, 0)))
    grid = lax.dynamic_slice_in_dim(grid, band * rows, rows + 2 * DEEP, 1)
    at_col = jnp.broadcast_to(jnp.arange(cols), grid.shape[1:])
    sides = jnp.stack([at_col == 0, at_col == cols - 1]).astype(jnp.int32)
    masks = jnp.concatenate([grid, sides], axis=0).astype(jnp.float32)
    masks = masks.reshape(masks.shape[0], -1)
    tile_cells = rows * tile_cols
    tile = velocity.reshape(2 * LAYERS, tile_cells)
    shown = (rows + 2 * EDGE) * cols
    deep = DEEP * cols
    f32 = jnp.float32
    vmem = pl.BlockSpec(memory_space=pltpu.VMEM)
    dma = pltpu.SemaphoreType.DMA
    pitch = 8
    while pitch < tile_cols + 2 * OSTEPS:
        pitch *= 2
    ocean_lanes = -(-(rows + 2 * OSTEPS) * pitch // 128) * 128
    result, ocean = pl.pallas_call(
        functools.partial(kernel, bands, freqs, cols),
        out_shape=(
            jax.ShapeDtypeStruct((DIR, cells), f32),
            jax.ShapeDtypeStruct((2 * LAYERS, tile_cells), f32),
        ),
        in_specs=[pl.BlockSpec(memory_space=pltpu.SMEM)] * 2 + [vmem] * 6,
        out_specs=(vmem, vmem),
        scratch_shapes=[
            pltpu.VMEM((2 * LAYERS, ocean_lanes), f32),
            pltpu.VMEM((DIR, cells + 2 * deep), f32),
            pltpu.VMEM((freqs, 2, tile_cells), f32),
            pltpu.VMEM((freqs, 2, tile_cells), f32),
            pltpu.VMEM((freqs, 2, tile_cells), f32),
            pltpu.VMEM((freqs, 2, tile_cells), f32),
            pltpu.VMEM((DIR, 4), f32),
            pltpu.VMEM((CYCLES, DIR, cells), f32),
            pltpu.VMEM((CYCLES, freqs, DIR, chunk), f32),
            pltpu.VMEM((CYCLES, freqs, DIR, chunk), f32),
            pltpu.VMEM((DIR, cells + 2 * SUB * cols), f32),
            pltpu.VMEM((2, shown), f32),
            pltpu.VMEM((freqs, 2, shown), f32),
            pltpu.VMEM((9, 2 * LAYERS, tile_cells), f32),
            pltpu.VMEM((2, cells + 2 * deep), f32),
            pltpu.VMEM((DIR, cells), f32),
            dma((2, 2)),
            dma((2, freqs)),
            dma((2, 2, freqs)),
            dma((2, 9)),
            dma((2, CYCLES, freqs)),
            dma((2, freqs)),
            dma((2, CYCLES, freqs)),
            dma((2, 2, freqs)),
        ],
        compiler_params=pltpu.CompilerParams(
            collective_id=0, has_side_effects=True, vmem_limit_bytes=60 * 1024 * 1024
        ),
    )(
        current_route,
        stokes_route,
        spectrum.reshape(DIR, cells),
        tile,
        gain_matrix,
        quad_matrix,
        masks,
        jnp.asarray(base),
    )
    return (result.reshape(1, DIR, rows, cols), ocean.reshape(velocity.shape))


def solution(mesh):
    return jax.shard_map(
        body,
        mesh=mesh,
        in_specs=(
            P("freq", None, "band", None),
            P(None, None, "band", "freq"),
            P(),
            P(),
            P(),
            P(),
            P(),
            P(),
        ),
        out_specs=(P("freq", None, "band", None), P(None, None, "band", "freq")),
        check_vma=False,
    )
```
